128 devices in a mesh: expert: 16 (over y, x), edata: 8 (over z, core).
Axes of the slice: x: 4, y: 4, z: 4, core: 2. Of those that a mesh axis runs over, the one named last changes fastest.
Arguments:
- out_grad: bfloat16 [131072, 4096], P(('expert', 'edata')), may hold values from -3.5 to 3.5
- hidden_saved: bfloat16 [131072, 768], P(('expert', 'edata')), may hold values from -6 to 6
- recv_counts: int32 [2048], P(('expert', 'edata')), may hold values from 1 to 64, as said below
- master_weight: float32 [65536, 768], P(('expert', 'edata'))
- moment_one: bfloat16 [65536, 768], P(('expert', 'edata')), may hold values from -4 to 4
- moment_two: bfloat16 [65536, 768], P(('expert', 'edata')), may hold values from 0.049804688 to 0.5
Outputs:
- new_master: float32 [65536, 768], P(('expert', 'edata'))
- new_moment_one: bfloat16 [65536, 768], P(('expert', 'edata'))
- new_moment_two: bfloat16 [65536, 768], P(('expert', 'edata'))
- scaled_weight: bfloat16 [65536, 768], P('expert')
- expert_peak: float32 [16], P('expert')
The draws below stay inside these ranges and needn't reach their ends.
Inputs may be any that keep to these rules, and one draw needn't show every extreme that they name: `recv_counts`: counts are skewed over experts; in every draw some pair fills all 64 slots.
All inputs are finite; a program needn't handle non-finite values. Where the reference program divides by a largest or mean magnitude, that divisor is 1e-20 or more.
Results may differ from the reference program's by a relative error of at most 0.001.
Values may be sent and summed in bfloat16 or wider, within the bound.
A program may use at most 128 MiB of HBM per device.

```python
import math
import jax
import jax.numpy as jnp
from jax import lax

D = 4096
FFN = 768
CAPACITY = 64
EXPERTS = 16
REPLICAS = 8


def draw_recv_counts(key, part):
    key_base = jax.random.fold_in(key, 11)
    key_heavy = jax.random.fold_in(key, 12)
    base = jax.random.randint(key_base, (EXPERTS, REPLICAS * EXPERTS), 1, CAPACITY + 1)
    heavy = jax.random.randint(key_heavy, (EXPERTS,), 0, 4) == 0
    counts = jnp.where(heavy[:, None], CAPACITY, base).reshape(-1).astype(jnp.int32)
    return counts.at[0].set(CAPACITY)


def draw_master_weight(key, part):
    rows = jnp.arange(EXPERTS * D) % D
    factor = 1.0 + 2.0 * rows.astype(jnp.float32) / float(max(D - 1, 1))
    values = jax.random.normal(key, (EXPERTS * D, FFN), jnp.float32)
    return (0.04 * values * factor[:, None]).astype(jnp.float32)


def with_spikes(entries, stream_key, source, target, blocks, factor):
    def block_of(axis_at):
        return (jnp.arange(entries.shape[axis_at]) // (entries.shape[axis_at] // blocks)).reshape((-1,) + (1,) * (entries.ndim - 1 - axis_at))

    near = jax.random.permutation(stream_key, blocks)[block_of(target)]
    far = (block_of(target) + blocks // 2) % blocks
    return jnp.where((block_of(source) == near) | (block_of(source) == far), factor * entries, entries)


def shard_levels(key, shape, cuts, smallest, largest):
    loudness, own = 1.0, jax.random.fold_in(key, 6)
    for axis_at, shards_of in cuts:
        heights = jnp.exp(jax.random.uniform(jax.random.fold_in(own, axis_at), (shards_of,), jnp.float32, smallest / len(cuts), largest / len(cuts)))
        loudness = loudness * jnp.repeat(heights, shape[axis_at] // shards_of).reshape([-1 if axis == axis_at else 1 for axis in range(len(shape))])
    return loudness


def noise(key, shape, scale, most, shards=(), dtype=jnp.bfloat16):
    loudness = shard_levels(key, shape, shards, -0.22, 0.18) if shards else 1.0
    values = jax.random.normal(key, shape, jnp.float32) * scale * loudness
    return jnp.minimum(jnp.maximum(values, -most), most).astype(dtype)


def gaussian_with(rng, shape, deviation, limit, pieces, heavy, kind=jnp.bfloat16):
    values = deviation * jax.random.normal(rng, shape, jnp.float32)
    if pieces:
        values = values * shard_levels(rng, shape, pieces, -0.22, 0.18)
    return jnp.clip(with_spikes(values, jax.random.fold_in(rng, 3), *heavy), -limit, limit).astype(kind)


def setup_inputs(seed: int = 0) -> dict:
    streams_of = jax.random.split(jax.random.key(seed), 7)
    out_grad = gaussian_with(streams_of[0], (REPLICAS * EXPERTS * EXPERTS * CAPACITY, D), 0.15, 3.5, ((0, 128),), (0, 1, 128, 5.5))
    hidden_saved = noise(streams_of[1], (EXPERTS * REPLICAS * EXPERTS * CAPACITY, FFN), 1.0, 6.0, ((0, 128),))
    recv_counts = draw_recv_counts(jax.random.fold_in(streams_of[6], 71), 0)
    master_weight = draw_master_weight(jax.random.fold_in(streams_of[6], 71), 0)
    moment_one = noise(streams_of[4], (EXPERTS * D, FFN), 1.0, 4.0, ((0, 128),))
    moment_two = jnp.clip(jnp.exp(math.log(0.5) - 2.306499 * jax.random.uniform(streams_of[5], (EXPERTS * D, FFN), jnp.float32) ** shard_levels(streams_of[5], (EXPERTS * D, FFN), ((0, 128),), -0.2, 0.2)), 0.049804688, 0.5).astype(jnp.bfloat16)
    return dict(out_grad=out_grad, hidden_saved=hidden_saved, recv_counts=recv_counts, master_weight=master_weight, moment_one=moment_one, moment_two=moment_two)


beta_one = 0.9
beta_two = 0.999
correct_one = 1.0 - 0.9 ** 5
correct_two = 1.0 - 0.999 ** 5
adam_eps = 1e-08
learn_rate = 0.05
weight_decay = 1.0
peak_eps = 1e-06

def reference(out_grad, hidden_saved, recv_counts, master_weight, moment_one, moment_two):
    grads_all = out_grad.reshape(EXPERTS, REPLICAS, EXPERTS, CAPACITY, D)
    hidden_all = hidden_saved.reshape(EXPERTS, REPLICAS, EXPERTS, CAPACITY, FFN)
    counts_all = recv_counts.reshape(EXPERTS, REPLICAS, EXPERTS)

    def one_expert(index):
        rows_in = lax.dynamic_index_in_dim(grads_all, index, 2, keepdims=False)
        rows_in = jnp.transpose(rows_in, (1, 0, 2, 3))
        hidden_in = lax.dynamic_index_in_dim(hidden_all, index, 0, keepdims=False)
        counts_in = lax.dynamic_index_in_dim(counts_all, index, 0, keepdims=False)
        slots = jnp.arange(CAPACITY).astype(jnp.int32)
        live = slots[None, None, :] < counts_in[:, :, None]
        masked = jnp.where(live[..., None], rows_in.astype(jnp.float32), jnp.float32(0.0))
        return jnp.einsum('rscd,rscf->df', masked, hidden_in.astype(jnp.float32))
    grad = lax.map(one_expert, jnp.arange(EXPERTS).astype(jnp.int32)).reshape(EXPERTS * D, FFN)
    first = beta_one * moment_one.astype(jnp.float32) + (1.0 - beta_one) * grad
    second = beta_two * moment_two.astype(jnp.float32) + (1.0 - beta_two) * grad * grad
    update = first / correct_one / (jnp.sqrt(second / correct_two) + adam_eps)
    new_master = master_weight - learn_rate * (update + weight_decay * master_weight)
    blocks = new_master.reshape(EXPERTS, D, FFN)
    expert_peak = lax.optimization_barrier(jnp.max(jnp.abs(blocks), axis=(1, 2)))
    scaled = (blocks / (expert_peak[:, None, None] + peak_eps)).astype(jnp.bfloat16)
    return (new_master, first.astype(jnp.bfloat16), second.astype(jnp.bfloat16), scaled.reshape(EXPERTS * D, FFN), expert_peak)
```

```python
import functools

import jax
import jax.numpy as jnp
from jax import lax
from jax.experimental import pallas as pl
from jax.experimental.pallas import tpu as pltpu
from jax.sharding import PartitionSpec as P

MESH = pl.DeviceIdType.MESH

beta_one = 0.9
beta_two = 0.999
correct_one = 1.0 - 0.9**5
correct_two = 1.0 - 0.999**5
adam_eps = 1e-08
learn_rate = 0.05
weight_decay = 1.0
peak_eps = 1e-06

D = 4096
FFN = 768
HALF = FFN // 2
NC = 8
AHEAD = 3


def exchange_kernel(
    x_ref, h_ref, cnt_ref, mw_ref, m1_ref, m2_ref,
    w_ref, m1o_ref, m2o_ref,
    F, RA, RB, H, HT, PB, DB, ZR, ZF, mw, m1, m2, nm, n1, n2,
    l1, s1, r1, s2, r2, l2, ds, dr, zs, zr, gs, gr, ls, isem,
):
    e = lax.axis_index("expert")
    k = lax.axis_index("edata")
    y, x = e // 4, lax.rem(e, 4)
    z, c = k // 2, lax.rem(k, 2)
    zp, zm, zo = lax.rem(z + 1, 4), lax.rem(z + 3, 4), lax.rem(z + 2, 4)
    sib = (e, 2 * z + 1 - c)
    up = (e, 2 * zp + c)
    down = (e, 2 * zm + c)
    hops = (1, 3, 2)

    def xdev(p):
        return (y * 4 + p, k)

    def ydev(p):
        return (p * 4 + x, k)

    def rc(src, dst, ssem, rsem, dev):
        return pltpu.make_async_remote_copy(
            src_ref=src, dst_ref=dst, send_sem=ssem, recv_sem=rsem,
            device_id=dev, device_id_type=MESH,
        )

    lc = pltpu.make_async_copy

    barrier = pltpu.get_barrier_semaphore()
    for d in hops:
        pl.semaphore_signal(barrier, inc=1, device_id=xdev(lax.rem(x + d, 4)), device_id_type=MESH)
        pl.semaphore_signal(barrier, inc=1, device_id=ydev(lax.rem(y + d, 4)), device_id_type=MESH)
    for dev in (sib, up, down):
        pl.semaphore_signal(barrier, inc=1, device_id=dev, device_id_type=MESH)

    ins = (
        lc(h_ref, H, isem.at[0]),
        lc(mw_ref, mw, isem.at[1]),
        lc(m1_ref, m1, isem.at[2]),
        lc(m2_ref, m2, isem.at[3]),
    )
    for cp in ins:
        cp.start()
    pl.semaphore_wait(barrier, 9)

    R = (RA, RB)
    own1 = (x, y)
    own2 = (y, x)

    def start1(j):
        base = 512 * lax.rem(j, 2) + 128 * (j // 2)

        def src(h, p, s):
            cols = pl.ds(pl.multiple_of(1024 * s + base, 128), 128)
            if h == 0:
                return x_ref.at[:, p, pl.ds(0, 32), cols]
            return x_ref.at[p, :, pl.ds(32, 32), cols]

        for i, d in enumerate(hops):
            for h in (0, 1):
                p = lax.rem(own1[h] + d, 4)
                for s in range(4):
                    rc(
                        src(h, p, s), R[h].at[j, :, own1[h], :, pl.ds(128 * s, 128)],
                        s1.at[h, j, i], r1.at[h, j, i], (xdev, ydev)[h](p),
                    ).start()
        for h in (0, 1):
            for s in range(4):
                lc(src(h, own1[h], s), R[h].at[j, :, own1[h], :, pl.ds(128 * s, 128)], l1.at[h, j]).start()

    def dst2(h, j):
        if h == 0:
            return F.at[j, y, :, pl.ds(0, 32)]
        return F.at[j, :, x, pl.ds(32, 32)]

    def start2(j):
        for h in (0, 1):
            mine = R[h].at[j, :, own1[h]]
            lc(mine, mine, l1.at[h, j]).wait()
            for i, d in enumerate(hops):
                got = R[h].at[j, :, lax.rem(own1[h] + 4 - d, 4)]
                rc(got, got, s1.at[h, j, i], r1.at[h, j, i], sib).wait_recv()
            for i, d in enumerate(hops):
                p = lax.rem(own2[h] + d, 4)
                rc(R[h].at[j, p], dst2(h, j), s2.at[h, j, i], r2.at[h, j, i], (ydev, xdev)[h](p)).start()
            lc(R[h].at[j, own2[h]], dst2(h, j), l2.at[h, j]).start()

    def got2(h, j, i):
        p = lax.rem(own2[h] + 4 - hops[i], 4)
        if h == 0:
            return F.at[j, p, :, pl.ds(0, 32)]
        return F.at[j, :, p, pl.ds(32, 32)]

    def multiply(j):
        for h in (0, 1):
            for i in range(3):
                g = got2(h, j, i)
                rc(g, g, s2.at[h, j, i], r2.at[h, j, i], sib).wait_recv()
            lc(R[h].at[j, own2[h]], dst2(h, j), l2.at[h, j]).wait()
        for n in range(2):
            a = F[j, :, :, :, pl.ds(256 * n, 256)].reshape(1024, 256)
            prod = jnp.dot(HT[...], a, preferred_element_type=jnp.float32)
            PB[j, 2 * n] = prod[:, :128]
            PB[j, 2 * n + 1] = prod[:, 128:]

    def to_sibling(j):
        return rc(PB.at[j], DB.at[j // 2], ds.at[j // 2], dr.at[j // 2], sib)

    def zcopies(j):
        q = j // 2
        lo, hi = pl.ds(0, HALF), pl.ds(HALF, HALF)
        return (
            rc(PB.at[j, zo, lo], ZR.at[q, 0], zs.at[q, 0], zr.at[q, 0], up),
            rc(PB.at[j, zo, hi], ZR.at[q, 1], zs.at[q, 1], zr.at[q, 1], down),
            rc(PB.at[j, zp, hi], ZF.at[q, 0, hi], zs.at[q, 2], zr.at[q, 2], up),
            rc(PB.at[j, zm, lo], ZF.at[q, 1, lo], zs.at[q, 3], zr.at[q, 3], down),
            rc(PB.at[j, zp, lo], ZF.at[q, 0, lo], zs.at[q, 4], zr.at[q, 4], up),
            rc(PB.at[j, zm, hi], ZF.at[q, 1, hi], zs.at[q, 5], zr.at[q, 5], down),
        )

    def reduce_one(j):
        q = j // 2
        to_sibling(j).wait_recv()
        cps = zcopies(j)
        PB[j, zo] = PB[j, zo] + DB[q, zo]
        cps[0].start()
        cps[1].start()
        PB[j, zp] = PB[j, zp] + DB[q, zp]
        cps[2].start()
        PB[j, zm] = PB[j, zm] + DB[q, zm]
        cps[3].start()
        PB[j, z] = PB[j, z] + DB[q, z]

    def reduce_two(j):
        q = j // 2
        cps = zcopies(j)
        cps[0].wait_recv()
        PB[j, zp, pl.ds(0, HALF)] = PB[j, zp, pl.ds(0, HALF)] + ZR[q, 0]
        cps[4].start()
        cps[1].wait_recv()
        PB[j, zm, pl.ds(HALF, HALF)] = PB[j, zm, pl.ds(HALF, HALF)] + ZR[q, 1]
        cps[5].start()

    def block(zz, q, first=0, rows=128):
        start = (2 * zz + c) * 512 + 128 * q + first
        return w_ref.at[pl.ds(pl.multiple_of(start, 64), rows)]

    def gcopies(q):
        own = nm.at[pl.ds(pl.multiple_of(128 * q, 128), 128)]
        return (
            rc(own, block(z, q), gs.at[q, 0], gr.at[q, 0], up),
            rc(own, block(z, q), gs.at[q, 1], gr.at[q, 1], down),
            rc(own, block(z, q), gs.at[q, 4], gr.at[q, 4], sib),
        )

    def lcopies(q):
        rows = pl.ds(pl.multiple_of(128 * q, 128), 128)
        return (
            lc(nm.at[rows], block(z, q), ls.at[q, 0]),
            lc(n1.at[rows], m1o_ref.at[rows], ls.at[q, 1]),
            lc(n2.at[rows], m2o_ref.at[rows], ls.at[q, 2]),
        )

    def finish(j):
        q = j // 2
        cps = zcopies(j)
        cps[2].wait_recv()
        cps[3].wait_recv()
        cps[4].wait_recv()
        cps[5].wait_recv()
        grad = (PB[j, z] + ZF[q, 0] + ZF[q, 1]).T
        rows = pl.ds(pl.multiple_of(128 * q, 128), 128)
        first = beta_one * m1[rows].astype(jnp.float32) + (1.0 - beta_one) * grad
        second = beta_two * m2[rows].astype(jnp.float32) + (1.0 - beta_two) * grad * grad
        update = first / correct_one / (jnp.sqrt(second / correct_two) + adam_eps)
        weight = mw[rows]
        nm[rows] = weight - learn_rate * (update + weight_decay * weight)
        n1[rows] = first.astype(jnp.bfloat16)
        n2[rows] = second.astype(jnp.bfloat16)
        for cp in gcopies(q) + lcopies(q):
            cp.start()

    def fcopies(q):
        return (
            rc(block(zm, q, 0, 64), block(zm, q, 0, 64), gs.at[q, 2], gr.at[q, 2], up),
            rc(block(zp, q, 64, 64), block(zp, q, 64, 64), gs.at[q, 3], gr.at[q, 3], down),
            rc(block(zm, q), block(zm, q), gs.at[q, 5], gr.at[q, 5], sib),
            rc(block(zp, q), block(zp, q), gs.at[q, 6], gr.at[q, 6], sib),
            rc(block(zo, q), block(zo, q), gs.at[q, 7], gr.at[q, 7], sib),
        )

    def forward_one(j):
        q = j // 2
        g, f = gcopies(q), fcopies(q)
        g[0].wait_recv()
        f[0].start()
        f[2].start()
        g[1].wait_recv()
        f[1].start()
        f[3].start()

    def forward_two(j):
        f = fcopies(j // 2)
        f[0].wait_recv()
        f[1].wait_recv()
        f[4].start()

    for j in range(AHEAD):
        start1(j)

    ins[0].wait()
    slot = lax.broadcasted_iota(jnp.int32, (64, FFN), 0)
    for s in range(8):
        parts = []
        for t in (2 * s, 2 * s + 1):
            rows = H[pl.ds(64 * t, 64)].astype(jnp.float32)
            parts.append(jnp.where(slot < cnt_ref[t], rows, 0.0))
        HT[:, pl.ds(128 * s, 128)] = jnp.concatenate(parts, axis=0).T.astype(jnp.bfloat16)
    for cp in ins[1:]:
        cp.wait()

    def step(t, carry):
        @pl.when(t < NC)
        def _():
            start2(t)

        @pl.when(t + AHEAD < NC)
        def _():
            start1(t + AHEAD)

        def stage(lag, fn):
            j = t - lag

            @pl.when((j >= 0) & (j < NC) & (lax.rem(j + 2 * NC, 2) == c))
            def _():
                fn(j)

        stage(4, forward_two)
        stage(3, forward_one)

        j = t - 1

        @pl.when((j >= 0) & (j < NC))
        def _():
            multiply(j)

            @pl.when(lax.rem(j, 2) != c)
            def _():
                to_sibling(j).start()

        stage(1, reduce_one)
        stage(2, reduce_two)
        stage(2, finish)
        return carry

    lax.fori_loop(0, NC + 4, step, 0)

    def drain(q, carry):
        f = fcopies(q)
        blocks = (z, zm, zp, zo)
        for i in range(4):
            start = (2 * blocks[i] + 1 - c) * 512 + 128 * q
            b = w_ref.at[pl.ds(pl.multiple_of(start, 128), 128)]
            rc(b, b, gs.at[q, 4 + i], gr.at[q, 4 + i], sib).wait_recv()
        for cp in gcopies(q) + f:
            cp.wait_send()
        for cp in lcopies(q):
            cp.wait()
        for cp in zcopies(2 * q + c):
            cp.wait_send()
        to_sibling(2 * q + 1 - c).wait_send()
        return carry

    lax.fori_loop(0, NC // 2, drain, 0)

    def drain_sends(j, carry):
        for h in (0, 1):
            for i in range(3):
                a = R[h].at[j, :, 0]
                rc(a, a, s1.at[h, j, i], r1.at[h, j, i], sib).wait_send()
                a = R[h].at[j, 0]
                rc(a, a, s2.at[h, j, i], r2.at[h, j, i], sib).wait_send()
        return carry

    lax.fori_loop(0, NC, drain_sends, 0)


def exchange(out_grad, hidden, counts, master, m1, m2):
    V, DMA = pltpu.VMEM, pltpu.SemaphoreType.DMA
    f32, bf16 = jnp.float32, jnp.bfloat16
    any_spec = pl.BlockSpec(memory_space=pl.ANY)
    rows = master.shape[0]
    return pl.pallas_call(
        exchange_kernel,
        name="exchange",
        out_shape=(
            jax.ShapeDtypeStruct((D, FFN), f32),
            jax.ShapeDtypeStruct((rows, FFN), bf16),
            jax.ShapeDtypeStruct((rows, FFN), bf16),
        ),
        in_specs=[any_spec, any_spec, pl.BlockSpec(memory_space=pltpu.SMEM), any_spec, any_spec, any_spec],
        out_specs=(any_spec, any_spec, any_spec),
        scratch_shapes=[
            V((NC, 4, 4, 64, 512), bf16),
            V((NC, 4, 4, 32, 512), bf16),
            V((NC, 4, 4, 32, 512), bf16),
            V((1024, FFN), bf16),
            V((FFN, 1024), bf16),
            V((NC, 4, FFN, 128), f32),
            V((NC // 2, 4, FFN, 128), f32),
            V((NC // 2, 2, HALF, 128), f32),
            V((NC // 2, 2, FFN, 128), f32),
            V((rows, FFN), f32),
            V((rows, FFN), bf16),
            V((rows, FFN), bf16),
            V((rows, FFN), f32),
            V((rows, FFN), bf16),
            V((rows, FFN), bf16),
            DMA((2, NC)),
            DMA((2, NC, 3)),
            DMA((2, NC, 3)),
            DMA((2, NC, 3)),
            DMA((2, NC, 3)),
            DMA((2, NC)),
            DMA((NC // 2,)),
            DMA((NC // 2,)),
            DMA((NC // 2, 6)),
            DMA((NC // 2, 6)),
            DMA((NC // 2, 8)),
            DMA((NC // 2, 8)),
            DMA((NC // 2, 3)),
            DMA((4,)),
        ],
        compiler_params=pltpu.CompilerParams(
            collective_id=0, has_side_effects=True, vmem_limit_bytes=62 << 20
        ),
    )(out_grad.reshape(4, 4, 64, D), hidden, counts, master, m1, m2)


BLOCKS = 8
ROWS = D // BLOCKS


def scale_kernel(w_ref, m1_ref, m2_ref, nm_ref, m1o_ref, m2o_ref, s_ref, peak_ref, wv, sv, v1, v2, isem, osem):
    k = lax.axis_index("edata")
    lc = pltpu.make_async_copy

    def load(b):
        return lc(w_ref.at[pl.ds(b * ROWS, ROWS)], wv.at[b], isem.at[b])

    for b in range(BLOCKS):
        load(b).start()
    small = (lc(m1_ref, v1, isem.at[BLOCKS]), lc(m2_ref, v2, isem.at[BLOCKS + 1]))
    for cp in small:
        cp.start()
    top = jnp.zeros((64, FFN), jnp.float32)
    for b in range(BLOCKS):
        load(b).wait()

        def biggest(i, best, b=b):
            return jnp.maximum(best, jnp.abs(wv[b, pl.ds(pl.multiple_of(64 * i, 64), 64)]))

        top = lax.fori_loop(0, ROWS // 64, biggest, top)
    outs = [lc(wv.at[k], nm_ref, osem.at[BLOCKS])]
    outs[0].start()
    for cp, v, o, i in ((small[0], v1, m1o_ref, 1), (small[1], v2, m2o_ref, 2)):
        cp.wait()
        outs.append(lc(v, o, osem.at[BLOCKS + i]))
        outs[-1].start()
    peak = jnp.max(top)
    peak_ref[0] = peak
    whole = jnp.full((8, FFN), peak + peak_eps, jnp.float32)
    shrink = jnp.where(whole > 2.0**100, jnp.float32(2.0**-64), jnp.float32(1.0))
    factor = 1.0 / (whole * shrink)
    for b in range(BLOCKS):
        def put(i, carry, b=b):
            rows = pl.ds(pl.multiple_of(64 * i, 64), 64)
            v = wv[b, rows].reshape(8, 8, FFN)
            sv[b, rows] = ((v * shrink) * factor).reshape(64, FFN).astype(jnp.bfloat16)
            return carry

        lax.fori_loop(0, ROWS // 64, put, 0)
        outs.append(lc(sv.at[b], s_ref.at[pl.ds(b * ROWS, ROWS)], osem.at[b]))
        outs[-1].start()
    for cp in outs:
        cp.wait()


def scale(w, m1, m2):
    V, DMA = pltpu.VMEM, pltpu.SemaphoreType.DMA
    f32, bf16 = jnp.float32, jnp.bfloat16
    any_spec = pl.BlockSpec(memory_space=pl.ANY)
    rows = m1.shape[0]
    return pl.pallas_call(
        scale_kernel,
        name="scale",
        out_shape=(
            jax.ShapeDtypeStruct((rows, FFN), f32),
            jax.ShapeDtypeStruct((rows, FFN), bf16),
            jax.ShapeDtypeStruct((rows, FFN), bf16),
            jax.ShapeDtypeStruct((D, FFN), bf16),
            jax.ShapeDtypeStruct((1,), f32),
        ),
        in_specs=[any_spec] * 3,
        out_specs=(any_spec,) * 4 + (pl.BlockSpec(memory_space=pltpu.SMEM),),
        scratch_shapes=[
            V((BLOCKS, ROWS, FFN), f32),
            V((BLOCKS, ROWS, FFN), bf16),
            V((rows, FFN), bf16),
            V((rows, FFN), bf16),
            DMA((BLOCKS + 2,)),
            DMA((BLOCKS + 3,)),
        ],
        compiler_params=pltpu.CompilerParams(vmem_limit_bytes=40 << 20),
    )(w, m1, m2)


def local(out_grad, hidden_saved, recv_counts, master_weight, moment_one, moment_two):
    w, n1, n2 = exchange(out_grad, hidden_saved, recv_counts, master_weight, moment_one, moment_two)
    new_master, n1, n2, scaled, peak = scale(w, n1, n2)
    return new_master, n1, n2, scaled, peak


def solution(mesh):
    placed = (
        P(("expert", "edata"), None),
        P(("expert", "edata"), None),
        P(("expert", "edata")),
        P(("expert", "edata"), None),
        P(("expert", "edata"), None),
        P(("expert", "edata"), None),
    )
    return jax.shard_map(
        local,
        mesh=mesh,
        in_specs=placed,
        out_specs=(
            P(("expert", "edata"), None),
            P(("expert", "edata"), None),
            P(("expert", "edata"), None),
            P("expert", None),
            P("expert"),
        ),
        check_vma=False,
    )
```

```python
import functools

import jax
import jax.numpy as jnp
from jax import lax
from jax.experimental import pallas as pl
from jax.experimental.pallas import tpu as pltpu
from jax.sharding import PartitionSpec as P

MESH = pl.DeviceIdType.MESH

beta_one = 0.9
beta_two = 0.999
correct_one = 1.0 - 0.9**5
correct_two = 1.0 - 0.999**5
adam_eps = 1e-08
learn_rate = 0.05
weight_decay = 1.0
peak_eps = 1e-06

D = 4096
FFN = 768
HALF = FFN // 2
NC = 8
AHEAD = 2
QN = NC // 2
EARLY = 96
EARLY_LAST = 48
LATE = 128 - EARLY
EN = (QN - 1) * EARLY + EARLY_LAST
LN = 128 * QN - EN
LA = (QN - 1) * LATE
LB = 128 - EARLY_LAST


def scale_factors(peak, rows):
    whole = jnp.full((rows, FFN), peak + peak_eps, jnp.float32)
    shrink = jnp.where(whole > 2.0**100, jnp.float32(2.0**-64), jnp.float32(1.0))
    return shrink, 1.0 / (whole * shrink)


def exchange_kernel(
    x_ref, h_ref, cnt_ref, mw_ref, m1_ref, m2_ref,
    w_ref, sl_ref, nmo_ref, m1o_ref, m2o_ref, pk_ref,
    F, RA, RB, H, HT, PB, DB, ZR, ZF, mw, m1, m2, nm, n1, n2, sl, PK, top,
    l1, s1, r1, s2, r2, l2, ds, dr, zs, zr, gs, gr, gl, ls, isem, ps, pr,
):
    e = lax.axis_index("expert")
    k = lax.axis_index("edata")
    y, x = e // 4, lax.rem(e, 4)
    z, c = k // 2, lax.rem(k, 2)
    zp, zm, zo = lax.rem(z + 1, 4), lax.rem(z + 3, 4), lax.rem(z + 2, 4)
    sib = (e, 2 * z + 1 - c)
    up = (e, 2 * zp + c)
    down = (e, 2 * zm + c)
    hops = (1, 3, 2)

    def xdev(p):
        return (y * 4 + p, k)

    def ydev(p):
        return (p * 4 + x, k)

    def rc(src, dst, ssem, rsem, dev):
        return pltpu.make_async_remote_copy(
            src_ref=src, dst_ref=dst, send_sem=ssem, recv_sem=rsem,
            device_id=dev, device_id_type=MESH,
        )

    lc = pltpu.make_async_copy

    barrier = pltpu.get_barrier_semaphore()
    for d in hops:
        pl.semaphore_signal(barrier, inc=1, device_id=xdev(lax.rem(x + d, 4)), device_id_type=MESH)
        pl.semaphore_signal(barrier, inc=1, device_id=ydev(lax.rem(y + d, 4)), device_id_type=MESH)
    for i in range(1, 8):
        dev = (e, lax.rem(k + i, 8))
        pl.semaphore_signal(barrier, inc=1, device_id=dev, device_id_type=MESH)

    ins = (
        lc(h_ref, H, isem.at[0]),
        lc(mw_ref, mw, isem.at[1]),
        lc(m1_ref, m1, isem.at[2]),
        lc(m2_ref, m2, isem.at[3]),
    )
    for cp in ins:
        cp.start()
    pl.semaphore_wait(barrier, 13)

    R = (RA, RB)
    own1 = (x, y)
    own2 = (y, x)

    def start1(j):
        base = 512 * lax.rem(j, 2) + 128 * (j // 2)

        def src(h, p, s):
            cols = pl.ds(pl.multiple_of(1024 * s + base, 128), 128)
            if h == 0:
                return x_ref.at[:, p, pl.ds(0, 32), cols]
            return x_ref.at[p, :, pl.ds(32, 32), cols]

        for i, d in enumerate(hops):
            for h in (0, 1):
                p = lax.rem(own1[h] + d, 4)
                for s in range(4):
                    rc(
                        src(h, p, s), R[h].at[j, :, own1[h], :, pl.ds(128 * s, 128)],
                        s1.at[h, j, i], r1.at[h, j, i], (xdev, ydev)[h](p),
                    ).start()
        for h in (0, 1):
            for s in range(4):
                lc(src(h, own1[h], s), R[h].at[j, :, own1[h], :, pl.ds(128 * s, 128)], l1.at[h, j]).start()

    def dst2(h, j):
        if h == 0:
            return F.at[j, y, :, pl.ds(0, 32)]
        return F.at[j, :, x, pl.ds(32, 32)]

    def start2(j):
        for h in (0, 1):
            mine = R[h].at[j, :, own1[h]]
            lc(mine, mine, l1.at[h, j]).wait()
            for i, d in enumerate(hops):
                got = R[h].at[j, :, lax.rem(own1[h] + 4 - d, 4)]
                rc(got, got, s1.at[h, j, i], r1.at[h, j, i], sib).wait_recv()
            for i, d in enumerate(hops):
                p = lax.rem(own2[h] + d, 4)
                rc(R[h].at[j, p], dst2(h, j), s2.at[h, j, i], r2.at[h, j, i], (ydev, xdev)[h](p)).start()
            lc(R[h].at[j, own2[h]], dst2(h, j), l2.at[h, j]).start()

    def got2(h, j, i):
        p = lax.rem(own2[h] + 4 - hops[i], 4)
        if h == 0:
            return F.at[j, p, :, pl.ds(0, 32)]
        return F.at[j, :, p, pl.ds(32, 32)]

    def multiply(j):
        for h in (0, 1):
            for i in range(3):
                g = got2(h, j, i)
                rc(g, g, s2.at[h, j, i], r2.at[h, j, i], sib).wait_recv()
            lc(R[h].at[j, own2[h]], dst2(h, j), l2.at[h, j]).wait()
        for n in range(2):
            a = F[j, :, :, :, pl.ds(256 * n, 256)].reshape(1024, 256)
            prod = jnp.dot(HT[...], a, preferred_element_type=jnp.float32)
            PB[j, 2 * n] = prod[:, :128]
            PB[j, 2 * n + 1] = prod[:, 128:]

    def to_sibling(j):
        return rc(PB.at[j], DB.at[j // 2], ds.at[j // 2], dr.at[j // 2], sib)

    def zcopies(j):
        q = j // 2
        lo, hi = pl.ds(0, HALF), pl.ds(HALF, HALF)
        return (
            rc(PB.at[j, zo, lo], ZR.at[q, 0], zs.at[q, 0], zr.at[q, 0], up),
            rc(PB.at[j, zo, hi], ZR.at[q, 1], zs.at[q, 1], zr.at[q, 1], down),
            rc(PB.at[j, zp, hi], ZF.at[q, 0, hi], zs.at[q, 2], zr.at[q, 2], up),
            rc(PB.at[j, zm, lo], ZF.at[q, 1, lo], zs.at[q, 3], zr.at[q, 3], down),
            rc(PB.at[j, zp, lo], ZF.at[q, 0, lo], zs.at[q, 4], zr.at[q, 4], up),
            rc(PB.at[j, zm, hi], ZF.at[q, 1, hi], zs.at[q, 5], zr.at[q, 5], down),
        )

    def reduce_one(j):
        q = j // 2
        to_sibling(j).wait_recv()
        cps = zcopies(j)
        PB[j, zo] = PB[j, zo] + DB[q, zo]
        cps[0].start()
        cps[1].start()
        PB[j, zp] = PB[j, zp] + DB[q, zp]
        cps[2].start()
        PB[j, zm] = PB[j, zm] + DB[q, zm]
        cps[3].start()
        PB[j, z] = PB[j, z] + DB[q, z]

    def reduce_two(j):
        q = j // 2
        cps = zcopies(j)
        cps[0].wait_recv()
        PB[j, zp, pl.ds(0, HALF)] = PB[j, zp, pl.ds(0, HALF)] + ZR[q, 0]
        cps[4].start()
        cps[1].wait_recv()
        PB[j, zm, pl.ds(HALF, HALF)] = PB[j, zm, pl.ds(HALF, HALF)] + ZR[q, 1]
        cps[5].start()

    def rows_of(q):
        return pl.ds(pl.multiple_of(128 * q, 128), 128)

    def part(g, last):
        if last is None:
            return w_ref, pl.multiple_of(EARLY * g, 8), EARLY, EARLY // 2
        return (
            (w_ref, (QN - 1) * EARLY, EARLY_LAST, EARLY_LAST // 2),
            (sl_ref, 0, LA, LA // 32 * 16),
            (sl_ref, LA, LB, (LB + 31) // 32 * 16),
        )[last]

    def block(kk, g, last, piece=0):
        ref, off, n, cut = part(g, last)
        first, count = ((0, n), (0, cut), (cut, n - cut))[piece]
        return ref.at[kk, pl.ds(off + first, count)]

    def gcopies(g, last=None):
        if last is None:
            own = nm.at[pl.ds(pl.multiple_of(128 * g, 128), EARLY)]
        else:
            own = (nm.at[pl.ds(128 * (QN - 1), EARLY_LAST)], sl.at[pl.ds(0, LA)], sl.at[pl.ds(LA, LB)])[last]
        b = block(k, g, last)
        return (
            rc(own, b, gs.at[g, 0], gr.at[g, 0], up),
            rc(own, b, gs.at[g, 1], gr.at[g, 1], down),
            rc(own, b, gs.at[g, 4], gr.at[g, 4], sib),
            lc(own, b, gl.at[g]),
        )

    def lcopies(q):
        rows = rows_of(q)
        return (
            lc(nm.at[rows], nmo_ref.at[rows], ls.at[q, 0]),
            lc(n1.at[rows], m1o_ref.at[rows], ls.at[q, 1]),
            lc(n2.at[rows], m2o_ref.at[rows], ls.at[q, 2]),
        )

    def finish(j):
        q = j // 2
        cps = zcopies(j)
        cps[2].wait_recv()
        cps[3].wait_recv()
        cps[4].wait_recv()
        cps[5].wait_recv()
        grad = (PB[j, z] + ZF[q, 0] + ZF[q, 1]).T
        rows = pl.ds(pl.multiple_of(128 * q, 128), 128)
        first = beta_one * m1[rows].astype(jnp.float32) + (1.0 - beta_one) * grad
        second = beta_two * m2[rows].astype(jnp.float32) + (1.0 - beta_two) * grad * grad
        update = first / correct_one / (jnp.sqrt(second / correct_two) + adam_eps)
        weight = mw[rows]
        weight = weight - learn_rate * (update + weight_decay * weight)
        nm[rows] = weight
        size = jnp.abs(weight)
        most = size[:8]
        for i in range(1, 16):
            most = jnp.maximum(most, size[8 * i : 8 * i + 8])
        top[...] = jnp.maximum(top[...], most)
        n1[rows] = first.astype(jnp.bfloat16)
        n2[rows] = second.astype(jnp.bfloat16)
        for cp in lcopies(q):
            cp.start()

        @pl.when(q < QN - 1)
        def _():
            for cp in gcopies(q):
                cp.start()

    def fcopies(g, last=None):
        km, kp, ko = 2 * zm + c, 2 * zp + c, 2 * zo + c
        lo, hi = block(km, g, last, 1), block(kp, g, last, 2)
        bm, bp, bo = block(km, g, last), block(kp, g, last), block(ko, g, last)
        return (
            rc(lo, lo, gs.at[g, 2], gr.at[g, 2], up),
            rc(hi, hi, gs.at[g, 3], gr.at[g, 3], down),
            rc(bm, bm, gs.at[g, 5], gr.at[g, 5], sib),
            rc(bp, bp, gs.at[g, 6], gr.at[g, 6], sib),
            rc(bo, bo, gs.at[g, 7], gr.at[g, 7], sib),
        )

    def forward_one(g, last=None):
        w, f = gcopies(g, last), fcopies(g, last)
        w[0].wait_recv()
        f[0].start()
        f[2].start()
        w[1].wait_recv()
        f[1].start()
        f[3].start()

    def forward_two(g, last=None):
        ko = 2 * zo + c
        f = fcopies(g, last)
        lo, hi = block(ko, g, last, 1), block(ko, g, last, 2)
        rc(lo, lo, gs.at[g, 2], gr.at[g, 2], up).wait_recv()
        rc(hi, hi, gs.at[g, 3], gr.at[g, 3], down).wait_recv()
        f[4].start()

    for j in range(AHEAD):
        start1(j)
    start2(0)
    start1(AHEAD)

    ins[0].wait()
    slot = lax.broadcasted_iota(jnp.int32, (64, FFN), 0)
    for s in range(8):
        parts = []
        for t in (2 * s, 2 * s + 1):
            rows = H[pl.ds(64 * t, 64)].astype(jnp.float32)
            parts.append(jnp.where(slot < cnt_ref[t], rows, 0.0))
        HT[:, pl.ds(128 * s, 128)] = jnp.concatenate(parts, axis=0).T.astype(jnp.bfloat16)
    for cp in ins[1:]:
        cp.wait()
    top[...] = jnp.zeros_like(top)

    def step(t, carry):
        @pl.when(t < NC)
        def _():
            start2(t)

        @pl.when(t + AHEAD < NC)
        def _():
            start1(t + AHEAD)

        def stage(lag, fn, last=NC):
            j = t - lag

            @pl.when((j >= 0) & (j < last) & (lax.rem(j + 2 * NC, 2) == c))
            def _():
                fn(j)

        stage(2, reduce_one)
        stage(3, finish)
        stage(5, lambda j: forward_two(j // 2), NC - 2)
        stage(4, lambda j: forward_one(j // 2), NC - 2)
        stage(2, reduce_two)
        j = t - 1

        @pl.when((j >= 0) & (j < NC))
        def _():
            multiply(j)

            @pl.when(lax.rem(j, 2) != c)
            def _():
                to_sibling(j).start()

        return carry

    lax.fori_loop(1, NC + 3, step, 0)

    tile = top[:, pl.ds(0, 128)]
    for i in range(1, FFN // 128):
        tile = jnp.maximum(tile, top[:, pl.ds(128 * i, 128)])
    PK[k] = tile
    pcopies = []
    for i in range(1, 8):
        p = lax.rem(k + i, 8)
        pcopies.append(rc(PK.at[k], PK.at[k], ps.at[i - 1], pr.at[i - 1], (e, p)))
        pcopies[-1].start()
    for cp in gcopies(QN - 1, 0):
        cp.start()
    for cp in pcopies:
        cp.wait_recv()
    peak = jnp.max(PK[...])
    pk_ref[...] = jnp.full((8, 128), peak, jnp.float32)
    shrink, factor = scale_factors(peak, 8)

    def put(start, first, n):
        rows = nm[pl.ds(first, n)].reshape(n // 8, 8, FFN)
        sl[pl.ds(start, n)] = ((rows * shrink) * factor).reshape(n, FFN).astype(jnp.bfloat16)

    for q in range(QN - 1):
        put(LATE * q, 128 * q + EARLY, LATE)
    for cp in gcopies(QN, 1):
        cp.start()
    put(LA, 128 * (QN - 1) + EARLY_LAST, LB)
    for cp in gcopies(QN + 1, 2):
        cp.start()
    for last in range(3):
        forward_one(QN - 1 + last, last)
    for last in range(3):
        forward_two(QN - 1 + last, last)

    def drain(g, last):
        blocks = (z, zm, zp, zo)
        for i in range(4):
            b = block(2 * blocks[i] + 1 - c, g, last)
            rc(b, b, gs.at[g, 4 + i], gr.at[g, 4 + i], sib).wait_recv()
        w = gcopies(g, last)
        for cp in w[:3] + fcopies(g, last):
            cp.wait_send()
        w[3].wait()

    for cp in pcopies:
        cp.wait_send()
    for g in range(QN - 1):
        drain(g, None)
    for last in range(3):
        drain(QN - 1 + last, last)
    for q in range(QN):
        for cp in lcopies(q):
            cp.wait()
        for cp in zcopies(2 * q + c):
            cp.wait_send()
        to_sibling(2 * q + 1 - c).wait_send()

    def drain_sends(j, carry):
        for h in (0, 1):
            for i in range(3):
                a = R[h].at[j, :, 0]
                rc(a, a, s1.at[h, j, i], r1.at[h, j, i], sib).wait_send()
                a = R[h].at[j, 0]
                rc(a, a, s2.at[h, j, i], r2.at[h, j, i], sib).wait_send()
        return carry

    lax.fori_loop(0, NC, drain_sends, 0)


def exchange(out_grad, hidden, counts, master, m1, m2):
    V, DMA = pltpu.VMEM, pltpu.SemaphoreType.DMA
    f32, bf16 = jnp.float32, jnp.bfloat16
    any_spec = pl.BlockSpec(memory_space=pl.ANY)
    rows = master.shape[0]
    return pl.pallas_call(
        exchange_kernel,
        name="exchange",
        out_shape=(
            jax.ShapeDtypeStruct((8, EN, FFN), f32),
            jax.ShapeDtypeStruct((8, LN, FFN), bf16),
            jax.ShapeDtypeStruct((rows, FFN), f32),
            jax.ShapeDtypeStruct((rows, FFN), bf16),
            jax.ShapeDtypeStruct((rows, FFN), bf16),
            jax.ShapeDtypeStruct((8, 128), f32),
        ),
        in_specs=[any_spec, any_spec, pl.BlockSpec(memory_space=pltpu.SMEM), any_spec, any_spec, any_spec],
        out_specs=(any_spec,) * 5 + (pl.BlockSpec(memory_space=pltpu.VMEM),),
        scratch_shapes=[
            V((NC, 4, 4, 64, 512), bf16),
            V((NC, 4, 4, 32, 512), bf16),
            V((NC, 4, 4, 32, 512), bf16),
            V((1024, FFN), bf16),
            V((FFN, 1024), bf16),
            V((NC, 4, FFN, 128), f32),
            V((NC // 2, 4, FFN, 128), f32),
            V((NC // 2, 2, HALF, 128), f32),
            V((NC // 2, 2, FFN, 128), f32),
            V((rows, FFN), f32),
            V((rows, FFN), bf16),
            V((rows, FFN), bf16),
            V((rows, FFN), f32),
            V((rows, FFN), bf16),
            V((rows, FFN), bf16),
            V((LN, FFN), bf16),
            V((8, 8, 128), f32),
            V((8, FFN), f32),
            DMA((2, NC)),
            DMA((2, NC, 3)),
            DMA((2, NC, 3)),
            DMA((2, NC, 3)),
            DMA((2, NC, 3)),
            DMA((2, NC)),
            DMA((NC // 2,)),
            DMA((NC // 2,)),
            DMA((NC // 2, 6)),
            DMA((NC // 2, 6)),
            DMA((QN + 2, 8)),
            DMA((QN + 2, 8)),
            DMA((QN + 2,)),
            DMA((QN, 3)),
            DMA((4,)),
            DMA((7,)),
            DMA((7,)),
        ],
        compiler_params=pltpu.CompilerParams(
            collective_id=0, has_side_effects=True, vmem_limit_bytes=62 << 20
        ),
    )(out_grad.reshape(4, 4, 64, D), hidden, counts, master, m1, m2)


BLOCKS = 8
ROWS = D // BLOCKS


def scale_kernel(
    w_ref, sl_ref, nmi_ref, m1_ref, m2_ref, pk_ref,
    nm_ref, m1o_ref, m2o_ref, s_ref, peak_ref,
    wv, sv, v0, v1, v2, isem, lsem, osem, ssem,
):
    lc = pltpu.make_async_copy
    early = [(128 * q, EARLY * q, EARLY) for q in range(QN - 1)] + [(128 * (QN - 1), EARLY * (QN - 1), EARLY_LAST)]
    late = [(128 * q + EARLY, LATE * q, LATE) for q in range(QN - 1)] + [(128 * (QN - 1) + EARLY_LAST, LA, LB)]

    def load(b):
        return [lc(w_ref.at[b], wv.at[b], isem.at[b])] + [
            lc(sl_ref.at[b, pl.ds(o, n)], sv.at[b, pl.ds(r, n)], lsem.at[b, i]) for i, (r, o, n) in enumerate(late)
        ]

    for b in range(BLOCKS):
        for cp in load(b):
            cp.start()
    small = (lc(nmi_ref, v0, ssem.at[0]), lc(m1_ref, v1, ssem.at[1]), lc(m2_ref, v2, ssem.at[2]))
    for cp in small:
        cp.start()
    peak = jnp.max(pk_ref[...])
    peak_ref[0] = peak
    shrink, factor = scale_factors(peak, 8)
    outs = []
    for b in range(BLOCKS):
        for cp in load(b):
            cp.wait()

        for r, o, n in early:
            v = wv[b, pl.ds(o, n)].reshape(n // 8, 8, FFN)
            sv[b, pl.ds(r, n)] = ((v * shrink) * factor).reshape(n, FFN).astype(jnp.bfloat16)
        outs.append(lc(sv.at[b], s_ref.at[pl.ds(b * ROWS, ROWS)], osem.at[b]))
        outs[-1].start()
    for i, (v, o) in enumerate(((v0, nm_ref), (v1, m1o_ref), (v2, m2o_ref))):
        small[i].wait()
        outs.append(lc(v, o, osem.at[BLOCKS + i]))
        outs[-1].start()
    for cp in outs:
        cp.wait()


def scale(w, sl, nm, m1, m2, pk):
    V, DMA = pltpu.VMEM, pltpu.SemaphoreType.DMA
    f32, bf16 = jnp.float32, jnp.bfloat16
    any_spec = pl.BlockSpec(memory_space=pl.ANY)
    rows = m1.shape[0]
    return pl.pallas_call(
        scale_kernel,
        name="scale",
        out_shape=(
            jax.ShapeDtypeStruct((rows, FFN), f32),
            jax.ShapeDtypeStruct((rows, FFN), bf16),
            jax.ShapeDtypeStruct((rows, FFN), bf16),
            jax.ShapeDtypeStruct((D, FFN), bf16),
            jax.ShapeDtypeStruct((1,), f32),
        ),
        in_specs=[any_spec] * 5 + [pl.BlockSpec(memory_space=pltpu.VMEM)],
        out_specs=(any_spec,) * 4 + (pl.BlockSpec(memory_space=pltpu.SMEM),),
        scratch_shapes=[
            V((BLOCKS, EN, FFN), f32),
            V((BLOCKS, ROWS, FFN), bf16),
            V((rows, FFN), f32),
            V((rows, FFN), bf16),
            V((rows, FFN), bf16),
            DMA((BLOCKS,)),
            DMA((BLOCKS, QN)),
            DMA((BLOCKS + 3,)),
            DMA((3,)),
        ],
        compiler_params=pltpu.CompilerParams(vmem_limit_bytes=63 << 20),
    )(w, sl, nm, m1, m2, pk)


def local(out_grad, hidden_saved, recv_counts, master_weight, moment_one, moment_two):
    w, sl, nm, n1, n2, pk = exchange(
        out_grad, hidden_saved, recv_counts, master_weight, moment_one, moment_two
    )
    return scale(w, sl, nm, n1, n2, pk)


def solution(mesh):
    placed = (
        P(("expert", "edata"), None),
        P(("expert", "edata"), None),
        P(("expert", "edata")),
        P(("expert", "edata"), None),
        P(("expert", "edata"), None),
        P(("expert", "edata"), None),
    )
    return jax.shard_map(
        local,
        mesh=mesh,
        in_specs=placed,
        out_specs=(
            P(("expert", "edata"), None),
            P(("expert", "edata"), None),
            P(("expert", "edata"), None),
            P("expert", None),
            P("expert"),
        ),
        check_vma=False,
    )
```

```python
import functools

import jax
import jax.numpy as jnp
from jax import lax
from jax.experimental import pallas as pl
from jax.experimental.pallas import tpu as pltpu
from jax.sharding import PartitionSpec as P

MESH = pl.DeviceIdType.MESH

beta_one = 0.9
beta_two = 0.999
correct_one = 1.0 - 0.9**5
correct_two = 1.0 - 0.999**5
adam_eps = 1e-08
learn_rate = 0.05
weight_decay = 1.0
peak_eps = 1e-06

D = 4096
FFN = 768
HALF = FFN // 2
NC = 8
AHEAD = 2
QN = NC // 2
EARLY = 64
EARLY_LAST = 64
LATE = 128 - EARLY
EN = (QN - 1) * EARLY + EARLY_LAST
LN = 128 * QN - EN
LA = (QN - 1) * LATE
LB = 128 - EARLY_LAST


def scale_factors(peak, rows):
    whole = jnp.full((rows, FFN), peak + peak_eps, jnp.float32)
    shrink = jnp.where(whole > 2.0**100, jnp.float32(2.0**-64), jnp.float32(1.0))
    return shrink, 1.0 / (whole * shrink)


def exchange_kernel(
    x_ref, h_ref, cnt_ref, mw_ref, m1_ref, m2_ref,
    w_ref, sl_ref, nmo_ref, m1o_ref, m2o_ref, pk_ref,
    F, RA, RB, H, HT, PB, DB, ZR, ZF, mw, m1, m2, nm, n1, n2, sl, PK, top,
    l1, s1, r1, s2, r2, l2, ds, dr, zs, zr, gs, gr, gl, ls, isem, ps, pr,
):
    e = lax.axis_index("expert")
    k = lax.axis_index("edata")
    y, x = e // 4, lax.rem(e, 4)
    z, c = k // 2, lax.rem(k, 2)
    zp, zm, zo = lax.rem(z + 1, 4), lax.rem(z + 3, 4), lax.rem(z + 2, 4)
    sib = (e, 2 * z + 1 - c)
    up = (e, 2 * zp + c)
    down = (e, 2 * zm + c)
    hops = (1, 3, 2)

    def xdev(p):
        return (y * 4 + p, k)

    def ydev(p):
        return (p * 4 + x, k)

    def rc(src, dst, ssem, rsem, dev):
        return pltpu.make_async_remote_copy(
            src_ref=src, dst_ref=dst, send_sem=ssem, recv_sem=rsem,
            device_id=dev, device_id_type=MESH,
        )

    lc = pltpu.make_async_copy

    barrier = pltpu.get_barrier_semaphore()
    for d in hops:
        pl.semaphore_signal(barrier, inc=1, device_id=xdev(lax.rem(x + d, 4)), device_id_type=MESH)
        pl.semaphore_signal(barrier, inc=1, device_id=ydev(lax.rem(y + d, 4)), device_id_type=MESH)
    for i in range(1, 8):
        dev = (e, lax.rem(k + i, 8))
        pl.semaphore_signal(barrier, inc=1, device_id=dev, device_id_type=MESH)

    ins = (
        lc(h_ref, H, isem.at[0]),
        lc(mw_ref, mw, isem.at[1]),
        lc(m1_ref, m1, isem.at[2]),
        lc(m2_ref, m2, isem.at[3]),
    )
    for cp in ins:
        cp.start()
    pl.semaphore_wait(barrier, 13)

    R = (RA, RB)
    own1 = (x, y)
    own2 = (y, x)

    def start1(j):
        base = 512 * lax.rem(j, 2) + 128 * (j // 2)

        def src(h, p, s):
            cols = pl.ds(pl.multiple_of(1024 * s + base, 128), 128)
            if h == 0:
                return x_ref.at[:, p, pl.ds(0, 32), cols]
            return x_ref.at[p, :, pl.ds(32, 32), cols]

        for i, d in enumerate(hops):
            for h in (0, 1):
                p = lax.rem(own1[h] + d, 4)
                for s in range(4):
                    rc(
                        src(h, p, s), R[h].at[j, :, own1[h], :, pl.ds(128 * s, 128)],
                        s1.at[h, j, i], r1.at[h, j, i], (xdev, ydev)[h](p),
                    ).start()
        for h in (0, 1):
            for s in range(4):
                lc(src(h, own1[h], s), R[h].at[j, :, own1[h], :, pl.ds(128 * s, 128)], l1.at[h, j]).start()

    def dst2(h, j):
        if h == 0:
            return F.at[j, y, :, pl.ds(0, 32)]
        return F.at[j, :, x, pl.ds(32, 32)]

    def start2(j):
        for h in (0, 1):
            mine = R[h].at[j, :, own1[h]]
            lc(mine, mine, l1.at[h, j]).wait()
            for i, d in enumerate(hops):
                got = R[h].at[j, :, lax.rem(own1[h] + 4 - d, 4)]
                rc(got, got, s1.at[h, j, i], r1.at[h, j, i], sib).wait_recv()
            for i, d in enumerate(hops):
                p = lax.rem(own2[h] + d, 4)
                rc(R[h].at[j, p], dst2(h, j), s2.at[h, j, i], r2.at[h, j, i], (ydev, xdev)[h](p)).start()
            lc(R[h].at[j, own2[h]], dst2(h, j), l2.at[h, j]).start()

    def got2(h, j, i):
        p = lax.rem(own2[h] + 4 - hops[i], 4)
        if h == 0:
            return F.at[j, p, :, pl.ds(0, 32)]
        return F.at[j, :, p, pl.ds(32, 32)]

    def multiply(j):
        for h in (0, 1):
            for i in range(3):
                g = got2(h, j, i)
                rc(g, g, s2.at[h, j, i], r2.at[h, j, i], sib).wait_recv()
            lc(R[h].at[j, own2[h]], dst2(h, j), l2.at[h, j]).wait()
        for n in range(2):
            a = F[j, :, :, :, pl.ds(256 * n, 256)].reshape(1024, 256)
            prod = jnp.dot(HT[...], a, preferred_element_type=jnp.float32)
            PB[j, 2 * n] = prod[:, :128]
            PB[j, 2 * n + 1] = prod[:, 128:]

    def to_sibling(j):
        return rc(PB.at[j], DB.at[j // 2], ds.at[j // 2], dr.at[j // 2], sib)

    def zcopies(j):
        q = j // 2
        lo, hi = pl.ds(0, HALF), pl.ds(HALF, HALF)
        return (
            rc(PB.at[j, zo, lo], ZR.at[q, 0], zs.at[q, 0], zr.at[q, 0], up),
            rc(PB.at[j, zo, hi], ZR.at[q, 1], zs.at[q, 1], zr.at[q, 1], down),
            rc(PB.at[j, zp, hi], ZF.at[q, 0, hi], zs.at[q, 2], zr.at[q, 2], up),
            rc(PB.at[j, zm, lo], ZF.at[q, 1, lo], zs.at[q, 3], zr.at[q, 3], down),
            rc(PB.at[j, zp, lo], ZF.at[q, 0, lo], zs.at[q, 4], zr.at[q, 4], up),
            rc(PB.at[j, zm, hi], ZF.at[q, 1, hi], zs.at[q, 5], zr.at[q, 5], down),
        )

    def reduce_one(j):
        q = j // 2
        to_sibling(j).wait_recv()
        cps = zcopies(j)
        PB[j, zo] = PB[j, zo] + DB[q, zo]
        cps[0].start()
        cps[1].start()
        PB[j, zp] = PB[j, zp] + DB[q, zp]
        cps[2].start()
        PB[j, zm] = PB[j, zm] + DB[q, zm]
        cps[3].start()
        PB[j, z] = PB[j, z] + DB[q, z]

    def reduce_two(j):
        q = j // 2
        cps = zcopies(j)
        cps[0].wait_recv()
        PB[j, zp, pl.ds(0, HALF)] = PB[j, zp, pl.ds(0, HALF)] + ZR[q, 0]
        cps[4].start()
        cps[1].wait_recv()
        PB[j, zm, pl.ds(HALF, HALF)] = PB[j, zm, pl.ds(HALF, HALF)] + ZR[q, 1]
        cps[5].start()

    def rows_of(q):
        return pl.ds(pl.multiple_of(128 * q, 128), 128)

    def part(g, last):
        if last is None:
            return w_ref, pl.multiple_of(EARLY * g, 8), EARLY, EARLY // 2
        return (
            (w_ref, (QN - 1) * EARLY, EARLY_LAST, EARLY_LAST // 2),
            (sl_ref, 0, LA, LA // 32 * 16),
            (sl_ref, LA, LB, (LB + 31) // 32 * 16),
        )[last]

    def block(kk, g, last, piece=0):
        ref, off, n, cut = part(g, last)
        first, count = ((0, n), (0, cut), (cut, n - cut))[piece]
        return ref.at[kk, pl.ds(off + first, count)]

    def gcopies(g, last=None):
        if last is None:
            own = nm.at[pl.ds(pl.multiple_of(128 * g, 128), EARLY)]
        else:
            own = (nm.at[pl.ds(128 * (QN - 1), EARLY_LAST)], sl.at[pl.ds(0, LA)], sl.at[pl.ds(LA, LB)])[last]
        b = block(k, g, last)
        return (
            rc(own, b, gs.at[g, 0], gr.at[g, 0], up),
            rc(own, b, gs.at[g, 1], gr.at[g, 1], down),
            rc(own, b, gs.at[g, 4], gr.at[g, 4], sib),
            lc(own, b, gl.at[g]),
        )

    def lcopies(q):
        rows = rows_of(q)
        return (
            lc(nm.at[rows], nmo_ref.at[rows], ls.at[q, 0]),
            lc(n1.at[rows], m1o_ref.at[rows], ls.at[q, 1]),
            lc(n2.at[rows], m2o_ref.at[rows], ls.at[q, 2]),
        )

    def finish(j):
        q = j // 2
        cps = zcopies(j)
        cps[2].wait_recv()
        cps[3].wait_recv()
        cps[4].wait_recv()
        cps[5].wait_recv()
        grad = (PB[j, z] + ZF[q, 0] + ZF[q, 1]).T
        rows = pl.ds(pl.multiple_of(128 * q, 128), 128)
        first = beta_one * m1[rows].astype(jnp.float32) + (1.0 - beta_one) * grad
        second = beta_two * m2[rows].astype(jnp.float32) + (1.0 - beta_two) * grad * grad
        update = first / correct_one / (jnp.sqrt(second / correct_two) + adam_eps)
        weight = mw[rows]
        weight = weight - learn_rate * (update + weight_decay * weight)
        nm[rows] = weight
        size = jnp.abs(weight)
        most = size[:8]
        for i in range(1, 16):
            most = jnp.maximum(most, size[8 * i : 8 * i + 8])
        top[...] = jnp.maximum(top[...], most)
        n1[rows] = first.astype(jnp.bfloat16)
        n2[rows] = second.astype(jnp.bfloat16)
        for cp in lcopies(q):
            cp.start()

        @pl.when(q < QN - 1)
        def _():
            for cp in gcopies(q):
                cp.start()

    def fcopies(g, last=None):
        km, kp, ko = 2 * zm + c, 2 * zp + c, 2 * zo + c
        lo, hi = block(km, g, last, 1), block(kp, g, last, 2)
        bm, bp, bo = block(km, g, last), block(kp, g, last), block(ko, g, last)
        return (
            rc(lo, lo, gs.at[g, 2], gr.at[g, 2], up),
            rc(hi, hi, gs.at[g, 3], gr.at[g, 3], down),
            rc(bm, bm, gs.at[g, 5], gr.at[g, 5], sib),
            rc(bp, bp, gs.at[g, 6], gr.at[g, 6], sib),
            rc(bo, bo, gs.at[g, 7], gr.at[g, 7], sib),
        )

    def forward_one(g, last=None):
        w, f = gcopies(g, last), fcopies(g, last)
        w[0].wait_recv()
        f[0].start()
        f[2].start()
        w[1].wait_recv()
        f[1].start()
        f[3].start()

    def forward_two(g, last=None):
        ko = 2 * zo + c
        f = fcopies(g, last)
        lo, hi = block(ko, g, last, 1), block(ko, g, last, 2)
        rc(lo, lo, gs.at[g, 2], gr.at[g, 2], up).wait_recv()
        rc(hi, hi, gs.at[g, 3], gr.at[g, 3], down).wait_recv()
        f[4].start()

    for j in range(AHEAD):
        start1(j)
    start2(0)
    start1(AHEAD)

    ins[0].wait()
    slot = lax.broadcasted_iota(jnp.int32, (64, FFN), 0)
    for s in range(8):
        parts = []
        for t in (2 * s, 2 * s + 1):
            rows = H[pl.ds(64 * t, 64)].astype(jnp.float32)
            parts.append(jnp.where(slot < cnt_ref[t], rows, 0.0))
        HT[:, pl.ds(128 * s, 128)] = jnp.concatenate(parts, axis=0).T.astype(jnp.bfloat16)
    for cp in ins[1:]:
        cp.wait()
    top[...] = jnp.zeros_like(top)

    def step(t, carry):
        @pl.when(t < NC)
        def _():
            start2(t)

        @pl.when(t + AHEAD < NC)
        def _():
            start1(t + AHEAD)

        def stage(lag, fn, last=NC):
            j = t - lag

            @pl.when((j >= 0) & (j < last) & (lax.rem(j + 2 * NC, 2) == c))
            def _():
                fn(j)

        stage(2, reduce_one)
        stage(3, finish)
        j = t - 1

        @pl.when((j >= 0) & (j < NC))
        def _():
            multiply(j)

            @pl.when(lax.rem(j, 2) != c)
            def _():
                to_sibling(j).start()

        stage(2, reduce_two)
        stage(5, lambda j: forward_two(j // 2), NC - 2)
        stage(4, lambda j: forward_one(j // 2), NC - 2)
        return carry

    lax.fori_loop(1, NC + 3, step, 0)

    tile = top[:, pl.ds(0, 128)]
    for i in range(1, FFN // 128):
        tile = jnp.maximum(tile, top[:, pl.ds(128 * i, 128)])
    PK[k] = tile
    pcopies = []
    for i in range(1, 8):
        p = lax.rem(k + i, 8)
        pcopies.append(rc(PK.at[k], PK.at[k], ps.at[i - 1], pr.at[i - 1], (e, p)))
        pcopies[-1].start()
    for cp in gcopies(QN - 1, 0):
        cp.start()
    for cp in pcopies:
        cp.wait_recv()
    peak = jnp.max(PK[...])
    pk_ref[...] = jnp.full((8, 128), peak, jnp.float32)
    shrink, factor = scale_factors(peak, 8)

    def put(start, first, n):
        rows = nm[pl.ds(first, n)].reshape(n // 8, 8, FFN)
        sl[pl.ds(start, n)] = ((rows * shrink) * factor).reshape(n, FFN).astype(jnp.bfloat16)

    for q in range(QN - 1):
        put(LATE * q, 128 * q + EARLY, LATE)
    for cp in gcopies(QN, 1):
        cp.start()
    put(LA, 128 * (QN - 1) + EARLY_LAST, LB)
    for cp in gcopies(QN + 1, 2):
        cp.start()
    for last in range(3):
        forward_one(QN - 1 + last, last)
    for last in range(3):
        forward_two(QN - 1 + last, last)

    def drain(g, last):
        blocks = (z, zm, zp, zo)
        for i in range(4):
            b = block(2 * blocks[i] + 1 - c, g, last)
            rc(b, b, gs.at[g, 4 + i], gr.at[g, 4 + i], sib).wait_recv()
        w = gcopies(g, last)
        for cp in w[:3] + fcopies(g, last):
            cp.wait_send()
        w[3].wait()

    for cp in pcopies:
        cp.wait_send()
    for g in range(QN - 1):
        drain(g, None)
    for last in range(3):
        drain(QN - 1 + last, last)
    for q in range(QN):
        for cp in lcopies(q):
            cp.wait()
        for cp in zcopies(2 * q + c):
            cp.wait_send()
        to_sibling(2 * q + 1 - c).wait_send()

    def drain_sends(j, carry):
        for h in (0, 1):
            for i in range(3):
                a = R[h].at[j, :, 0]
                rc(a, a, s1.at[h, j, i], r1.at[h, j, i], sib).wait_send()
                a = R[h].at[j, 0]
                rc(a, a, s2.at[h, j, i], r2.at[h, j, i], sib).wait_send()
        return carry

    lax.fori_loop(0, NC, drain_sends, 0)


def exchange(out_grad, hidden, counts, master, m1, m2):
    V, DMA = pltpu.VMEM, pltpu.SemaphoreType.DMA
    f32, bf16 = jnp.float32, jnp.bfloat16
    any_spec = pl.BlockSpec(memory_space=pl.ANY)
    rows = master.shape[0]
    return pl.pallas_call(
        exchange_kernel,
        name="exchange",
        out_shape=(
            jax.ShapeDtypeStruct((8, EN, FFN), f32),
            jax.ShapeDtypeStruct((8, LN, FFN), bf16),
            jax.ShapeDtypeStruct((rows, FFN), f32),
            jax.ShapeDtypeStruct((rows, FFN), bf16),
            jax.ShapeDtypeStruct((rows, FFN), bf16),
            jax.ShapeDtypeStruct((8, 128), f32),
        ),
        in_specs=[any_spec, any_spec, pl.BlockSpec(memory_space=pltpu.SMEM), any_spec, any_spec, any_spec],
        out_specs=(any_spec,) * 5 + (pl.BlockSpec(memory_space=pltpu.VMEM),),
        scratch_shapes=[
            V((NC, 4, 4, 64, 512), bf16),
            V((NC, 4, 4, 32, 512), bf16),
            V((NC, 4, 4, 32, 512), bf16),
            V((1024, FFN), bf16),
            V((FFN, 1024), bf16),
            V((NC, 4, FFN, 128), f32),
            V((NC // 2, 4, FFN, 128), f32),
            V((NC // 2, 2, HALF, 128), f32),
            V((NC // 2, 2, FFN, 128), f32),
            V((rows, FFN), f32),
            V((rows, FFN), bf16),
            V((rows, FFN), bf16),
            V((rows, FFN), f32),
            V((rows, FFN), bf16),
            V((rows, FFN), bf16),
            V((LN, FFN), bf16),
            V((8, 8, 128), f32),
            V((8, FFN), f32),
            DMA((2, NC)),
            DMA((2, NC, 3)),
            DMA((2, NC, 3)),
            DMA((2, NC, 3)),
            DMA((2, NC, 3)),
            DMA((2, NC)),
            DMA((NC // 2,)),
            DMA((NC // 2,)),
            DMA((NC // 2, 6)),
            DMA((NC // 2, 6)),
            DMA((QN + 2, 8)),
            DMA((QN + 2, 8)),
            DMA((QN + 2,)),
            DMA((QN, 3)),
            DMA((4,)),
            DMA((7,)),
            DMA((7,)),
        ],
        compiler_params=pltpu.CompilerParams(
            collective_id=0, has_side_effects=True, vmem_limit_bytes=62 << 20
        ),
    )(out_grad.reshape(4, 4, 64, D), hidden, counts, master, m1, m2)


BLOCKS = 8
ROWS = D // BLOCKS


def scale_kernel(
    w_ref, sl_ref, nmi_ref, m1_ref, m2_ref, pk_ref,
    nm_ref, m1o_ref, m2o_ref, s_ref, peak_ref,
    wv, sv, v0, v1, v2, isem, lsem, osem, ssem,
):
    lc = pltpu.make_async_copy
    early = [(128 * q, EARLY * q, EARLY) for q in range(QN - 1)] + [(128 * (QN - 1), EARLY * (QN - 1), EARLY_LAST)]
    late = [(128 * q + EARLY, LATE * q, LATE) for q in range(QN - 1)] + [(128 * (QN - 1) + EARLY_LAST, LA, LB)]

    def load(b):
        return [lc(w_ref.at[b], wv.at[b], isem.at[b])] + [
            lc(sl_ref.at[b, pl.ds(o, n)], sv.at[b, pl.ds(r, n)], lsem.at[b, i]) for i, (r, o, n) in enumerate(late)
        ]

    small = (lc(nmi_ref, v0, ssem.at[0]), lc(m1_ref, v1, ssem.at[1]), lc(m2_ref, v2, ssem.at[2]))
    for cp in small:
        cp.start()
    for b in range(BLOCKS):
        for cp in load(b):
            cp.start()
    peak = jnp.max(pk_ref[...])
    peak_ref[0] = peak
    shrink, factor = scale_factors(peak, 8)
    outs = []
    for i, (v, o) in enumerate(((v0, nm_ref), (v1, m1o_ref), (v2, m2o_ref))):
        small[i].wait()
        outs.append(lc(v, o, osem.at[BLOCKS + i]))
        outs[-1].start()
    for b in range(BLOCKS):
        for cp in load(b):
            cp.wait()

        for r, o, n in early:
            v = wv[b, pl.ds(o, n)].reshape(n // 8, 8, FFN)
            sv[b, pl.ds(r, n)] = ((v * shrink) * factor).reshape(n, FFN).astype(jnp.bfloat16)
        outs.append(lc(sv.at[b], s_ref.at[pl.ds(b * ROWS, ROWS)], osem.at[b]))
        outs[-1].start()
    for cp in outs:
        cp.wait()


def scale(w, sl, nm, m1, m2, pk):
    V, DMA = pltpu.VMEM, pltpu.SemaphoreType.DMA
    f32, bf16 = jnp.float32, jnp.bfloat16
    any_spec = pl.BlockSpec(memory_space=pl.ANY)
    rows = m1.shape[0]
    return pl.pallas_call(
        scale_kernel,
        name="scale",
        out_shape=(
            jax.ShapeDtypeStruct((rows, FFN), f32),
            jax.ShapeDtypeStruct((rows, FFN), bf16),
            jax.ShapeDtypeStruct((rows, FFN), bf16),
            jax.ShapeDtypeStruct((D, FFN), bf16),
            jax.ShapeDtypeStruct((1,), f32),
        ),
        in_specs=[any_spec] * 5 + [pl.BlockSpec(memory_space=pltpu.VMEM)],
        out_specs=(any_spec,) * 4 + (pl.BlockSpec(memory_space=pltpu.SMEM),),
        scratch_shapes=[
            V((BLOCKS, EN, FFN), f32),
            V((BLOCKS, ROWS, FFN), bf16),
            V((rows, FFN), f32),
            V((rows, FFN), bf16),
            V((rows, FFN), bf16),
            DMA((BLOCKS,)),
            DMA((BLOCKS, QN)),
            DMA((BLOCKS + 3,)),
            DMA((3,)),
        ],
        compiler_params=pltpu.CompilerParams(vmem_limit_bytes=63 << 20),
    )(w, sl, nm, m1, m2, pk)


def local(out_grad, hidden_saved, recv_counts, master_weight, moment_one, moment_two):
    w, sl, nm, n1, n2, pk = exchange(
        out_grad, hidden_saved, recv_counts, master_weight, moment_one, moment_two
    )
    return scale(w, sl, nm, n1, n2, pk)


def solution(mesh):
    placed = (
        P(("expert", "edata"), None),
        P(("expert", "edata"), None),
        P(("expert", "edata")),
        P(("expert", "edata"), None),
        P(("expert", "edata"), None),
        P(("expert", "edata"), None),
    )
    return jax.shard_map(
        local,
        mesh=mesh,
        in_specs=placed,
        out_specs=(
            P(("expert", "edata"), None),
            P(("expert", "edata"), None),
            P(("expert", "edata"), None),
            P("expert", None),
            P("expert"),
        ),
        check_vma=False,
    )
```

```python
import functools

import jax
import jax.numpy as jnp
from jax import lax
from jax.experimental import pallas as pl
from jax.experimental.pallas import tpu as pltpu
from jax.sharding import PartitionSpec as P

MESH = pl.DeviceIdType.MESH

beta_one = 0.9
beta_two = 0.999
correct_one = 1.0 - 0.9**5
correct_two = 1.0 - 0.999**5
adam_eps = 1e-08
learn_rate = 0.05
weight_decay = 1.0
peak_eps = 1e-06

D = 4096
FFN = 768
HALF = FFN // 2
NC = 8
AHEAD = 2
QN = NC // 2
QF = 2
EARLY = 112
EARLY_LAST = 32
LATE = 128 - EARLY
EN = QF * EARLY + EARLY_LAST
LN = 128 * QN - EN
LA = QF * LATE + (QN - 1 - QF) * 128
LB = 128 - EARLY_LAST


def scale_factors(peak, rows):
    whole = jnp.full((rows, FFN), peak + peak_eps, jnp.float32)
    shrink = jnp.where(whole > 2.0**100, jnp.float32(2.0**-64), jnp.float32(1.0))
    return shrink, 1.0 / (whole * shrink)


def exchange_kernel(
    x_ref, h_ref, cnt_ref, mw_ref, m1_ref, m2_ref,
    w_ref, sl_ref, nmo_ref, m1o_ref, m2o_ref, pk_ref,
    F, RA, RB, H, HT, PB, DB, ZR, ZF, mw, m1, m2, nm, n1, n2, sl, PK, top,
    l1, s1, r1, s2, r2, l2, ds, dr, zs, zr, gs, gr, gl, ls, isem, ps, pr,
):
    e = lax.axis_index("expert")
    k = lax.axis_index("edata")
    y, x = e // 4, lax.rem(e, 4)
    z, c = k // 2, lax.rem(k, 2)
    zp, zm, zo = lax.rem(z + 1, 4), lax.rem(z + 3, 4), lax.rem(z + 2, 4)
    sib = (e, 2 * z + 1 - c)
    up = (e, 2 * zp + c)
    down = (e, 2 * zm + c)
    hops = (1, 3, 2)

    def xdev(p):
        return (y * 4 + p, k)

    def ydev(p):
        return (p * 4 + x, k)

    def rc(src, dst, ssem, rsem, dev):
        return pltpu.make_async_remote_copy(
            src_ref=src, dst_ref=dst, send_sem=ssem, recv_sem=rsem,
            device_id=dev, device_id_type=MESH,
        )

    lc = pltpu.make_async_copy

    barrier = pltpu.get_barrier_semaphore()
    for d in hops:
        pl.semaphore_signal(barrier, inc=1, device_id=xdev(lax.rem(x + d, 4)), device_id_type=MESH)
        pl.semaphore_signal(barrier, inc=1, device_id=ydev(lax.rem(y + d, 4)), device_id_type=MESH)
    for i in range(1, 8):
        dev = (e, lax.rem(k + i, 8))
        pl.semaphore_signal(barrier, inc=1, device_id=dev, device_id_type=MESH)

    ins = (
        lc(h_ref, H, isem.at[0]),
        lc(mw_ref, mw, isem.at[1]),
        lc(m1_ref, m1, isem.at[2]),
        lc(m2_ref, m2, isem.at[3]),
    )
    for cp in ins:
        cp.start()
    pl.semaphore_wait(barrier, 13)

    R = (RA, RB)
    own1 = (x, y)
    own2 = (y, x)

    def start1(j):
        base = 512 * lax.rem(j, 2) + 128 * (j // 2)

        def src(h, p, s):
            cols = pl.ds(pl.multiple_of(1024 * s + base, 128), 128)
            if h == 0:
                return x_ref.at[:, p, pl.ds(0, 32), cols]
            return x_ref.at[p, :, pl.ds(32, 32), cols]

        for i, d in enumerate(hops):
            for h in (0, 1):
                p = lax.rem(own1[h] + d, 4)
                for s in range(4):
                    rc(
                        src(h, p, s), R[h].at[j, :, own1[h], :, pl.ds(128 * s, 128)],
                        s1.at[h, j, i], r1.at[h, j, i], (xdev, ydev)[h](p),
                    ).start()
        for h in (0, 1):
            for s in range(4):
                lc(src(h, own1[h], s), R[h].at[j, :, own1[h], :, pl.ds(128 * s, 128)], l1.at[h, j]).start()

    def dst2(h, j):
        if h == 0:
            return F.at[j, y, :, pl.ds(0, 32)]
        return F.at[j, :, x, pl.ds(32, 32)]

    def start2(j):
        for h in (0, 1):
            mine = R[h].at[j, :, own1[h]]
            lc(mine, mine, l1.at[h, j]).wait()
            for i, d in enumerate(hops):
                got = R[h].at[j, :, lax.rem(own1[h] + 4 - d, 4)]
                rc(got, got, s1.at[h, j, i], r1.at[h, j, i], sib).wait_recv()
            for i, d in enumerate(hops):
                p = lax.rem(own2[h] + d, 4)
                rc(R[h].at[j, p], dst2(h, j), s2.at[h, j, i], r2.at[h, j, i], (ydev, xdev)[h](p)).start()
            lc(R[h].at[j, own2[h]], dst2(h, j), l2.at[h, j]).start()

    def got2(h, j, i):
        p = lax.rem(own2[h] + 4 - hops[i], 4)
        if h == 0:
            return F.at[j, p, :, pl.ds(0, 32)]
        return F.at[j, :, p, pl.ds(32, 32)]

    def multiply(j):
        for h in (0, 1):
            for i in range(3):
                g = got2(h, j, i)
                rc(g, g, s2.at[h, j, i], r2.at[h, j, i], sib).wait_recv()
            lc(R[h].at[j, own2[h]], dst2(h, j), l2.at[h, j]).wait()
        for n in range(2):
            a = F[j, :, :, :, pl.ds(256 * n, 256)].reshape(1024, 256)
            prod = jnp.dot(HT[...], a, preferred_element_type=jnp.float32)
            PB[j, 2 * n] = prod[:, :128]
            PB[j, 2 * n + 1] = prod[:, 128:]

    def to_sibling(j):
        return rc(PB.at[j], DB.at[j // 2], ds.at[j // 2], dr.at[j // 2], sib)

    def zcopies(j):
        q = j // 2
        lo, hi = pl.ds(0, HALF), pl.ds(HALF, HALF)
        return (
            rc(PB.at[j, zo, lo], ZR.at[q, 0], zs.at[q, 0], zr.at[q, 0], up),
            rc(PB.at[j, zo, hi], ZR.at[q, 1], zs.at[q, 1], zr.at[q, 1], down),
            rc(PB.at[j, zp, hi], ZF.at[q, 0, hi], zs.at[q, 2], zr.at[q, 2], up),
            rc(PB.at[j, zm, lo], ZF.at[q, 1, lo], zs.at[q, 3], zr.at[q, 3], down),
            rc(PB.at[j, zp, lo], ZF.at[q, 0, lo], zs.at[q, 4], zr.at[q, 4], up),
            rc(PB.at[j, zm, hi], ZF.at[q, 1, hi], zs.at[q, 5], zr.at[q, 5], down),
        )

    def reduce_one(j):
        q = j // 2
        to_sibling(j).wait_recv()
        cps = zcopies(j)
        PB[j, zo] = PB[j, zo] + DB[q, zo]
        cps[0].start()
        cps[1].start()
        PB[j, zp] = PB[j, zp] + DB[q, zp]
        cps[2].start()
        PB[j, zm] = PB[j, zm] + DB[q, zm]
        cps[3].start()
        PB[j, z] = PB[j, z] + DB[q, z]

    def reduce_two(j):
        q = j // 2
        cps = zcopies(j)
        cps[0].wait_recv()
        PB[j, zp, pl.ds(0, HALF)] = PB[j, zp, pl.ds(0, HALF)] + ZR[q, 0]
        cps[4].start()
        cps[1].wait_recv()
        PB[j, zm, pl.ds(HALF, HALF)] = PB[j, zm, pl.ds(HALF, HALF)] + ZR[q, 1]
        cps[5].start()

    def rows_of(q):
        return pl.ds(pl.multiple_of(128 * q, 128), 128)

    def part(g, last):
        if last is None:
            return w_ref, pl.multiple_of(EARLY * g, 8), EARLY, EARLY // 2
        return (
            (w_ref, QF * EARLY, EARLY_LAST, EARLY_LAST // 2),
            (sl_ref, 0, LA, LA // 32 * 16),
            (sl_ref, LA, LB, (LB + 31) // 32 * 16),
        )[last]

    def block(kk, g, last, piece=0):
        ref, off, n, cut = part(g, last)
        first, count = ((0, n), (0, cut), (cut, n - cut))[piece]
        return ref.at[kk, pl.ds(off + first, count)]

    def gcopies(g, last=None):
        if last is None:
            own = nm.at[pl.ds(pl.multiple_of(128 * g, 128), EARLY)]
        else:
            own = (nm.at[pl.ds(128 * (QN - 1), EARLY_LAST)], sl.at[pl.ds(0, LA)], sl.at[pl.ds(LA, LB)])[last]
        b = block(k, g, last)
        return (
            rc(own, b, gs.at[g, 0], gr.at[g, 0], up),
            rc(own, b, gs.at[g, 1], gr.at[g, 1], down),
            rc(own, b, gs.at[g, 4], gr.at[g, 4], sib),
            lc(own, b, gl.at[g]),
        )

    def lcopies(q):
        rows = rows_of(q)
        return (
            lc(nm.at[rows], nmo_ref.at[rows], ls.at[q, 0]),
            lc(n1.at[rows], m1o_ref.at[rows], ls.at[q, 1]),
            lc(n2.at[rows], m2o_ref.at[rows], ls.at[q, 2]),
        )

    def finish(j):
        q = j // 2
        cps = zcopies(j)
        cps[2].wait_recv()
        cps[3].wait_recv()
        cps[4].wait_recv()
        cps[5].wait_recv()
        grad = (PB[j, z] + ZF[q, 0] + ZF[q, 1]).T
        rows = pl.ds(pl.multiple_of(128 * q, 128), 128)
        first = beta_one * m1[rows].astype(jnp.float32) + (1.0 - beta_one) * grad
        second = beta_two * m2[rows].astype(jnp.float32) + (1.0 - beta_two) * grad * grad
        update = first / correct_one / (jnp.sqrt(second / correct_two) + adam_eps)
        weight = mw[rows]
        weight = weight - learn_rate * (update + weight_decay * weight)
        nm[rows] = weight
        size = jnp.abs(weight)
        most = size[:8]
        for i in range(1, 16):
            most = jnp.maximum(most, size[8 * i : 8 * i + 8])
        top[...] = jnp.maximum(top[...], most)
        n1[rows] = first.astype(jnp.bfloat16)
        n2[rows] = second.astype(jnp.bfloat16)
        for cp in lcopies(q):
            cp.start()

        @pl.when(q < QF)
        def _():
            for cp in gcopies(q):
                cp.start()

    def fcopies(g, last=None):
        km, kp, ko = 2 * zm + c, 2 * zp + c, 2 * zo + c
        lo, hi = block(km, g, last, 1), block(kp, g, last, 2)
        bm, bp, bo = block(km, g, last), block(kp, g, last), block(ko, g, last)
        return (
            rc(lo, lo, gs.at[g, 2], gr.at[g, 2], up),
            rc(hi, hi, gs.at[g, 3], gr.at[g, 3], down),
            rc(bm, bm, gs.at[g, 5], gr.at[g, 5], sib),
            rc(bp, bp, gs.at[g, 6], gr.at[g, 6], sib),
            rc(bo, bo, gs.at[g, 7], gr.at[g, 7], sib),
        )

    def forward_one(g, last=None):
        w, f = gcopies(g, last), fcopies(g, last)
        w[0].wait_recv()
        f[0].start()
        f[2].start()
        w[1].wait_recv()
        f[1].start()
        f[3].start()

    def forward_two(g, last=None):
        ko = 2 * zo + c
        f = fcopies(g, last)
        lo, hi = block(ko, g, last, 1), block(ko, g, last, 2)
        rc(lo, lo, gs.at[g, 2], gr.at[g, 2], up).wait_recv()
        rc(hi, hi, gs.at[g, 3], gr.at[g, 3], down).wait_recv()
        f[4].start()

    for j in range(AHEAD):
        start1(j)
    start2(0)
    start1(AHEAD)

    ins[0].wait()
    slot = lax.broadcasted_iota(jnp.int32, (64, FFN), 0)
    for s in range(8):
        parts = []
        for t in (2 * s, 2 * s + 1):
            rows = H[pl.ds(64 * t, 64)].astype(jnp.float32)
            parts.append(jnp.where(slot < cnt_ref[t], rows, 0.0))
        HT[:, pl.ds(128 * s, 128)] = jnp.concatenate(parts, axis=0).T.astype(jnp.bfloat16)
    for cp in ins[1:]:
        cp.wait()
    top[...] = jnp.zeros_like(top)

    def step(t, carry):
        @pl.when(t < NC)
        def _():
            start2(t)

        @pl.when(t + AHEAD < NC)
        def _():
            start1(t + AHEAD)

        def stage(lag, fn, last=NC):
            j = t - lag

            @pl.when((j >= 0) & (j < last) & (lax.rem(j + 2 * NC, 2) == c))
            def _():
                fn(j)

        stage(2, reduce_one)
        stage(3, finish)
        j = t - 1

        @pl.when((j >= 0) & (j < NC))
        def _():
            multiply(j)

            @pl.when(lax.rem(j, 2) != c)
            def _():
                to_sibling(j).start()

        stage(2, reduce_two)
        stage(5, lambda j: forward_two(j // 2), 2 * QF)
        stage(4, lambda j: forward_one(j // 2), 2 * QF)
        return carry

    lax.fori_loop(1, NC + 3, step, 0)

    tile = top[:, pl.ds(0, 128)]
    for i in range(1, FFN // 128):
        tile = jnp.maximum(tile, top[:, pl.ds(128 * i, 128)])
    PK[k] = tile
    pcopies = []
    for i in range(1, 8):
        p = lax.rem(k + i, 8)
        pcopies.append(rc(PK.at[k], PK.at[k], ps.at[i - 1], pr.at[i - 1], (e, p)))
        pcopies[-1].start()
    for cp in gcopies(QF, 0):
        cp.start()
    for cp in pcopies:
        cp.wait_recv()
    peak = jnp.max(PK[...])
    pk_ref[...] = jnp.full((8, 128), peak, jnp.float32)
    shrink, factor = scale_factors(peak, 8)

    def put(start, first, n):
        rows = nm[pl.ds(first, n)].reshape(n // 8, 8, FFN)
        sl[pl.ds(start, n)] = ((rows * shrink) * factor).reshape(n, FFN).astype(jnp.bfloat16)

    for q in range(QF):
        put(LATE * q, 128 * q + EARLY, LATE)
    for q in range(QF, QN - 1):
        put(LATE * QF + 128 * (q - QF), 128 * q, 128)
    for cp in gcopies(QF + 1, 1):
        cp.start()
    put(LA, 128 * (QN - 1) + EARLY_LAST, LB)
    for cp in gcopies(QF + 2, 2):
        cp.start()
    for last in range(3):
        forward_one(QF + last, last)
    for last in range(3):
        forward_two(QF + last, last)

    def drain(g, last):
        blocks = (z, zm, zp, zo)
        for i in range(4):
            b = block(2 * blocks[i] + 1 - c, g, last)
            rc(b, b, gs.at[g, 4 + i], gr.at[g, 4 + i], sib).wait_recv()
        w = gcopies(g, last)
        for cp in w[:3] + fcopies(g, last):
            cp.wait_send()
        w[3].wait()

    for cp in pcopies:
        cp.wait_send()
    for g in range(QF):
        drain(g, None)
    for last in range(3):
        drain(QF + last, last)
    for q in range(QN):
        for cp in lcopies(q):
            cp.wait()
        for cp in zcopies(2 * q + c):
            cp.wait_send()
        to_sibling(2 * q + 1 - c).wait_send()

    def drain_sends(j, carry):
        for h in (0, 1):
            for i in range(3):
                a = R[h].at[j, :, 0]
                rc(a, a, s1.at[h, j, i], r1.at[h, j, i], sib).wait_send()
                a = R[h].at[j, 0]
                rc(a, a, s2.at[h, j, i], r2.at[h, j, i], sib).wait_send()
        return carry

    lax.fori_loop(0, NC, drain_sends, 0)


def exchange(out_grad, hidden, counts, master, m1, m2):
    V, DMA = pltpu.VMEM, pltpu.SemaphoreType.DMA
    f32, bf16 = jnp.float32, jnp.bfloat16
    any_spec = pl.BlockSpec(memory_space=pl.ANY)
    rows = master.shape[0]
    return pl.pallas_call(
        exchange_kernel,
        name="exchange",
        out_shape=(
            jax.ShapeDtypeStruct((8, EN, FFN), f32),
            jax.ShapeDtypeStruct((8, LN, FFN), bf16),
            jax.ShapeDtypeStruct((rows, FFN), f32),
            jax.ShapeDtypeStruct((rows, FFN), bf16),
            jax.ShapeDtypeStruct((rows, FFN), bf16),
            jax.ShapeDtypeStruct((8, 128), f32),
        ),
        in_specs=[any_spec, any_spec, pl.BlockSpec(memory_space=pltpu.SMEM), any_spec, any_spec, any_spec],
        out_specs=(any_spec,) * 5 + (pl.BlockSpec(memory_space=pltpu.VMEM),),
        scratch_shapes=[
            V((NC, 4, 4, 64, 512), bf16),
            V((NC, 4, 4, 32, 512), bf16),
            V((NC, 4, 4, 32, 512), bf16),
            V((1024, FFN), bf16),
            V((FFN, 1024), bf16),
            V((NC, 4, FFN, 128), f32),
            V((NC // 2, 4, FFN, 128), f32),
            V((NC // 2, 2, HALF, 128), f32),
            V((NC // 2, 2, FFN, 128), f32),
            V((rows, FFN), f32),
            V((rows, FFN), bf16),
            V((rows, FFN), bf16),
            V((rows, FFN), f32),
            V((rows, FFN), bf16),
            V((rows, FFN), bf16),
            V((LN, FFN), bf16),
            V((8, 8, 128), f32),
            V((8, FFN), f32),
            DMA((2, NC)),
            DMA((2, NC, 3)),
            DMA((2, NC, 3)),
            DMA((2, NC, 3)),
            DMA((2, NC, 3)),
            DMA((2, NC)),
            DMA((NC // 2,)),
            DMA((NC // 2,)),
            DMA((NC // 2, 6)),
            DMA((NC // 2, 6)),
            DMA((QN + 2, 8)),
            DMA((QN + 2, 8)),
            DMA((QN + 2,)),
            DMA((QN, 3)),
            DMA((4,)),
            DMA((7,)),
            DMA((7,)),
        ],
        compiler_params=pltpu.CompilerParams(
            collective_id=0, has_side_effects=True, vmem_limit_bytes=62 << 20
        ),
    )(out_grad.reshape(4, 4, 64, D), hidden, counts, master, m1, m2)


BLOCKS = 8
ROWS = D // BLOCKS


def scale_kernel(
    w_ref, sl_ref, nmi_ref, m1_ref, m2_ref, pk_ref,
    nm_ref, m1o_ref, m2o_ref, s_ref, peak_ref,
    wv, sv, v0, v1, v2, isem, lsem, osem, ssem,
):
    lc = pltpu.make_async_copy
    early = [(128 * q, EARLY * q, EARLY) for q in range(QF)] + [(128 * (QN - 1), EARLY * QF, EARLY_LAST)]
    late = [(128 * q + EARLY, LATE * q, LATE) for q in range(QF)] + [
        (128 * q, LATE * QF + 128 * (q - QF), 128) for q in range(QF, QN - 1)
    ] + [(128 * (QN - 1) + EARLY_LAST, LA, LB)]

    def load(b):
        return [lc(w_ref.at[b], wv.at[b], isem.at[b])] + [
            lc(sl_ref.at[b, pl.ds(o, n)], sv.at[b, pl.ds(r, n)], lsem.at[b, i]) for i, (r, o, n) in enumerate(late)
        ]

    small = (lc(nmi_ref, v0, ssem.at[0]), lc(m1_ref, v1, ssem.at[1]), lc(m2_ref, v2, ssem.at[2]))
    for cp in small:
        cp.start()
    for b in range(BLOCKS):
        for cp in load(b):
            cp.start()
    peak = jnp.max(pk_ref[...])
    peak_ref[0] = peak
    shrink, factor = scale_factors(peak, 8)
    outs = []
    for i, (v, o) in enumerate(((v0, nm_ref), (v1, m1o_ref), (v2, m2o_ref))):
        small[i].wait()
        outs.append(lc(v, o, osem.at[BLOCKS + i]))
        outs[-1].start()
    for b in range(BLOCKS):
        for cp in load(b):
            cp.wait()

        for r, o, n in early:
            v = wv[b, pl.ds(o, n)].reshape(n // 8, 8, FFN)
            sv[b, pl.ds(r, n)] = ((v * shrink) * factor).reshape(n, FFN).astype(jnp.bfloat16)
        outs.append(lc(sv.at[b], s_ref.at[pl.ds(b * ROWS, ROWS)], osem.at[b]))
        outs[-1].start()
    for cp in outs:
        cp.wait()


def scale(w, sl, nm, m1, m2, pk):
    V, DMA = pltpu.VMEM, pltpu.SemaphoreType.DMA
    f32, bf16 = jnp.float32, jnp.bfloat16
    any_spec = pl.BlockSpec(memory_space=pl.ANY)
    rows = m1.shape[0]
    return pl.pallas_call(
        scale_kernel,
        name="scale",
        out_shape=(
            jax.ShapeDtypeStruct((rows, FFN), f32),
            jax.ShapeDtypeStruct((rows, FFN), bf16),
            jax.ShapeDtypeStruct((rows, FFN), bf16),
            jax.ShapeDtypeStruct((D, FFN), bf16),
            jax.ShapeDtypeStruct((1,), f32),
        ),
        in_specs=[any_spec] * 5 + [pl.BlockSpec(memory_space=pltpu.VMEM)],
        out_specs=(any_spec,) * 4 + (pl.BlockSpec(memory_space=pltpu.SMEM),),
        scratch_shapes=[
            V((BLOCKS, EN, FFN), f32),
            V((BLOCKS, ROWS, FFN), bf16),
            V((rows, FFN), f32),
            V((rows, FFN), bf16),
            V((rows, FFN), bf16),
            DMA((BLOCKS,)),
            DMA((BLOCKS, QN)),
            DMA((BLOCKS + 3,)),
            DMA((3,)),
        ],
        compiler_params=pltpu.CompilerParams(vmem_limit_bytes=63 << 20),
    )(w, sl, nm, m1, m2, pk)


def local(out_grad, hidden_saved, recv_counts, master_weight, moment_one, moment_two):
    w, sl, nm, n1, n2, pk = exchange(
        out_grad, hidden_saved, recv_counts, master_weight, moment_one, moment_two
    )
    return scale(w, sl, nm, n1, n2, pk)


def solution(mesh):
    placed = (
        P(("expert", "edata"), None),
        P(("expert", "edata"), None),
        P(("expert", "edata")),
        P(("expert", "edata"), None),
        P(("expert", "edata"), None),
        P(("expert", "edata"), None),
    )
    return jax.shard_map(
        local,
        mesh=mesh,
        in_specs=placed,
        out_specs=(
            P(("expert", "edata"), None),
            P(("expert", "edata"), None),
            P(("expert", "edata"), None),
            P("expert", None),
            P("expert"),
        ),
        check_vma=False,
    )
```

```python
import functools

import jax
import jax.numpy as jnp
from jax import lax
from jax.experimental import pallas as pl
from jax.experimental.pallas import tpu as pltpu
from jax.sharding import PartitionSpec as P

MESH = pl.DeviceIdType.MESH

beta_one = 0.9
beta_two = 0.999
correct_one = 1.0 - 0.9**5
correct_two = 1.0 - 0.999**5
adam_eps = 1e-08
learn_rate = 0.05
weight_decay = 1.0
peak_eps = 1e-06

D = 4096
FFN = 768
HALF = FFN // 2
NC = 8
AHEAD = 2
QN = NC // 2
QF = 2
EARLY = 112
EARLY_LAST = 64
LATE = 128 - EARLY
EN = QF * EARLY + EARLY_LAST
LN = 128 * QN - EN
LA = QF * LATE + (QN - 1 - QF) * 128
LB = 128 - EARLY_LAST


def scale_factors(peak, rows):
    whole = jnp.full((rows, FFN), peak + peak_eps, jnp.float32)
    shrink = jnp.where(whole > 2.0**100, jnp.float32(2.0**-64), jnp.float32(1.0))
    return shrink, 1.0 / (whole * shrink)


def exchange_kernel(
    x_ref, h_ref, cnt_ref, mw_ref, m1_ref, m2_ref,
    w_ref, sl_ref, nmo_ref, m1o_ref, m2o_ref, pk_ref,
    F, RA, RB, H, HT, PB, DB, ZR, ZF, mw, m1, m2, nm, n1, n2, sl, PK, top,
    l1, s1, r1, s2, r2, l2, ds, dr, zs, zr, gs, gr, gl, ls, isem, ps, pr,
):
    e = lax.axis_index("expert")
    k = lax.axis_index("edata")
    y, x = e // 4, lax.rem(e, 4)
    z, c = k // 2, lax.rem(k, 2)
    zp, zm, zo = lax.rem(z + 1, 4), lax.rem(z + 3, 4), lax.rem(z + 2, 4)
    sib = (e, 2 * z + 1 - c)
    up = (e, 2 * zp + c)
    down = (e, 2 * zm + c)
    hops = (1, 3, 2)

    def xdev(p):
        return (y * 4 + p, k)

    def ydev(p):
        return (p * 4 + x, k)

    def rc(src, dst, ssem, rsem, dev):
        return pltpu.make_async_remote_copy(
            src_ref=src, dst_ref=dst, send_sem=ssem, recv_sem=rsem,
            device_id=dev, device_id_type=MESH,
        )

    lc = pltpu.make_async_copy

    barrier = pltpu.get_barrier_semaphore()
    for d in hops:
        pl.semaphore_signal(barrier, inc=1, device_id=xdev(lax.rem(x + d, 4)), device_id_type=MESH)
        pl.semaphore_signal(barrier, inc=1, device_id=ydev(lax.rem(y + d, 4)), device_id_type=MESH)
    for i in range(1, 8):
        dev = (e, lax.rem(k + i, 8))
        pl.semaphore_signal(barrier, inc=1, device_id=dev, device_id_type=MESH)

    ins = (
        lc(h_ref, H, isem.at[0]),
        lc(mw_ref, mw, isem.at[1]),
        lc(m1_ref, m1, isem.at[2]),
        lc(m2_ref, m2, isem.at[3]),
    )
    for cp in ins:
        cp.start()
    pl.semaphore_wait(barrier, 13)

    R = (RA, RB)
    own1 = (x, y)
    own2 = (y, x)

    def start1(j):
        base = 512 * lax.rem(j, 2) + 128 * (j // 2)

        def src(h, p, s):
            cols = pl.ds(pl.multiple_of(1024 * s + base, 128), 128)
            if h == 0:
                return x_ref.at[:, p, pl.ds(0, 32), cols]
            return x_ref.at[p, :, pl.ds(32, 32), cols]

        for i, d in enumerate(hops):
            for h in (0, 1):
                p = lax.rem(own1[h] + d, 4)
                for s in range(4):
                    rc(
                        src(h, p, s), R[h].at[j, :, own1[h], :, pl.ds(128 * s, 128)],
                        s1.at[h, j, i], r1.at[h, j, i], (xdev, ydev)[h](p),
                    ).start()
        for h in (0, 1):
            for s in range(4):
                lc(src(h, own1[h], s), R[h].at[j, :, own1[h], :, pl.ds(128 * s, 128)], l1.at[h, j]).start()

    def dst2(h, j):
        if h == 0:
            return F.at[j, y, :, pl.ds(0, 32)]
        return F.at[j, :, x, pl.ds(32, 32)]

    def start2(j):
        for h in (0, 1):
            mine = R[h].at[j, :, own1[h]]
            lc(mine, mine, l1.at[h, j]).wait()
            for i, d in enumerate(hops):
                got = R[h].at[j, :, lax.rem(own1[h] + 4 - d, 4)]
                rc(got, got, s1.at[h, j, i], r1.at[h, j, i], sib).wait_recv()
            for i, d in enumerate(hops):
                p = lax.rem(own2[h] + d, 4)
                rc(R[h].at[j, p], dst2(h, j), s2.at[h, j, i], r2.at[h, j, i], (ydev, xdev)[h](p)).start()
            lc(R[h].at[j, own2[h]], dst2(h, j), l2.at[h, j]).start()

    def got2(h, j, i):
        p = lax.rem(own2[h] + 4 - hops[i], 4)
        if h == 0:
            return F.at[j, p, :, pl.ds(0, 32)]
        return F.at[j, :, p, pl.ds(32, 32)]

    def multiply(j):
        for h in (0, 1):
            for i in range(3):
                g = got2(h, j, i)
                rc(g, g, s2.at[h, j, i], r2.at[h, j, i], sib).wait_recv()
            lc(R[h].at[j, own2[h]], dst2(h, j), l2.at[h, j]).wait()
        for n in range(2):
            a = F[j, :, :, :, pl.ds(256 * n, 256)].reshape(1024, 256)
            prod = jnp.dot(HT[...], a, preferred_element_type=jnp.float32)
            PB[j, 2 * n] = prod[:, :128]
            PB[j, 2 * n + 1] = prod[:, 128:]

    def to_sibling(j):
        return rc(PB.at[j], DB.at[j // 2], ds.at[j // 2], dr.at[j // 2], sib)

    def zcopies(j):
        q = j // 2
        lo, hi = pl.ds(0, HALF), pl.ds(HALF, HALF)
        return (
            rc(PB.at[j, zo, lo], ZR.at[q, 0], zs.at[q, 0], zr.at[q, 0], up),
            rc(PB.at[j, zo, hi], ZR.at[q, 1], zs.at[q, 1], zr.at[q, 1], down),
            rc(PB.at[j, zp, hi], ZF.at[q, 0, hi], zs.at[q, 2], zr.at[q, 2], up),
            rc(PB.at[j, zm, lo], ZF.at[q, 1, lo], zs.at[q, 3], zr.at[q, 3], down),
            rc(PB.at[j, zp, lo], ZF.at[q, 0, lo], zs.at[q, 4], zr.at[q, 4], up),
            rc(PB.at[j, zm, hi], ZF.at[q, 1, hi], zs.at[q, 5], zr.at[q, 5], down),
        )

    def reduce_one(j):
        q = j // 2
        to_sibling(j).wait_recv()
        cps = zcopies(j)
        PB[j, zo] = PB[j, zo] + DB[q, zo]
        cps[0].start()
        cps[1].start()
        PB[j, zp] = PB[j, zp] + DB[q, zp]
        cps[2].start()
        PB[j, zm] = PB[j, zm] + DB[q, zm]
        cps[3].start()
        PB[j, z] = PB[j, z] + DB[q, z]

    def reduce_two(j):
        q = j // 2
        cps = zcopies(j)
        cps[0].wait_recv()
        PB[j, zp, pl.ds(0, HALF)] = PB[j, zp, pl.ds(0, HALF)] + ZR[q, 0]
        cps[4].start()
        cps[1].wait_recv()
        PB[j, zm, pl.ds(HALF, HALF)] = PB[j, zm, pl.ds(HALF, HALF)] + ZR[q, 1]
        cps[5].start()

    def rows_of(q):
        return pl.ds(pl.multiple_of(128 * q, 128), 128)

    def part(g, last):
        if last is None:
            return w_ref, pl.multiple_of(EARLY * g, 8), EARLY, EARLY // 2
        return (
            (w_ref, QF * EARLY, EARLY_LAST, EARLY_LAST // 2),
            (sl_ref, 0, LA, LA // 32 * 16),
            (sl_ref, LA, LB, (LB + 31) // 32 * 16),
        )[last]

    def block(kk, g, last, piece=0):
        ref, off, n, cut = part(g, last)
        first, count = ((0, n), (0, cut), (cut, n - cut))[piece]
        return ref.at[kk, pl.ds(off + first, count)]

    def gcopies(g, last=None):
        if last is None:
            own = nm.at[pl.ds(pl.multiple_of(128 * g, 128), EARLY)]
        else:
            own = (nm.at[pl.ds(128 * (QN - 1), EARLY_LAST)], sl.at[pl.ds(0, LA)], sl.at[pl.ds(LA, LB)])[last]
        b = block(k, g, last)
        return (
            rc(own, b, gs.at[g, 0], gr.at[g, 0], up),
            rc(own, b, gs.at[g, 1], gr.at[g, 1], down),
            rc(own, b, gs.at[g, 4], gr.at[g, 4], sib),
            lc(own, b, gl.at[g]),
        )

    def lcopies(q):
        rows = rows_of(q)
        return (
            lc(nm.at[rows], nmo_ref.at[rows], ls.at[q, 0]),
            lc(n1.at[rows], m1o_ref.at[rows], ls.at[q, 1]),
            lc(n2.at[rows], m2o_ref.at[rows], ls.at[q, 2]),
        )

    def finish(j):
        q = j // 2
        cps = zcopies(j)
        cps[2].wait_recv()
        cps[3].wait_recv()
        cps[4].wait_recv()
        cps[5].wait_recv()
        grad = (PB[j, z] + ZF[q, 0] + ZF[q, 1]).T
        rows = pl.ds(pl.multiple_of(128 * q, 128), 128)
        first = beta_one * m1[rows].astype(jnp.float32) + (1.0 - beta_one) * grad
        second = beta_two * m2[rows].astype(jnp.float32) + (1.0 - beta_two) * grad * grad
        update = first / correct_one / (jnp.sqrt(second / correct_two) + adam_eps)
        weight = mw[rows]
        weight = weight - learn_rate * (update + weight_decay * weight)
        nm[rows] = weight
        size = jnp.abs(weight)
        most = size[:8]
        for i in range(1, 16):
            most = jnp.maximum(most, size[8 * i : 8 * i + 8])
        top[...] = jnp.maximum(top[...], most)
        n1[rows] = first.astype(jnp.bfloat16)
        n2[rows] = second.astype(jnp.bfloat16)
        for cp in lcopies(q):
            cp.start()

        @pl.when(q < QF)
        def _():
            for cp in gcopies(q):
                cp.start()

    def fcopies(g, last=None):
        km, kp, ko = 2 * zm + c, 2 * zp + c, 2 * zo + c
        lo, hi = block(km, g, last, 1), block(kp, g, last, 2)
        bm, bp, bo = block(km, g, last), block(kp, g, last), block(ko, g, last)
        return (
            rc(lo, lo, gs.at[g, 2], gr.at[g, 2], up),
            rc(hi, hi, gs.at[g, 3], gr.at[g, 3], down),
            rc(bm, bm, gs.at[g, 5], gr.at[g, 5], sib),
            rc(bp, bp, gs.at[g, 6], gr.at[g, 6], sib),
            rc(bo, bo, gs.at[g, 7], gr.at[g, 7], sib),
        )

    def forward_one(g, last=None):
        w, f = gcopies(g, last), fcopies(g, last)
        w[0].wait_recv()
        f[0].start()
        f[2].start()
        w[1].wait_recv()
        f[1].start()
        f[3].start()

    def forward_two(g, last=None):
        ko = 2 * zo + c
        f = fcopies(g, last)
        lo, hi = block(ko, g, last, 1), block(ko, g, last, 2)
        rc(lo, lo, gs.at[g, 2], gr.at[g, 2], up).wait_recv()
        rc(hi, hi, gs.at[g, 3], gr.at[g, 3], down).wait_recv()
        f[4].start()

    for j in range(AHEAD):
        start1(j)
    start2(0)
    start1(AHEAD)

    ins[0].wait()
    slot = lax.broadcasted_iota(jnp.int32, (64, FFN), 0)
    for s in range(8):
        parts = []
        for t in (2 * s, 2 * s + 1):
            rows = H[pl.ds(64 * t, 64)].astype(jnp.float32)
            parts.append(jnp.where(slot < cnt_ref[t], rows, 0.0))
        HT[:, pl.ds(128 * s, 128)] = jnp.concatenate(parts, axis=0).T.astype(jnp.bfloat16)
    for cp in ins[1:]:
        cp.wait()
    top[...] = jnp.zeros_like(top)

    def step(t, carry):
        @pl.when(t < NC)
        def _():
            start2(t)

        @pl.when(t + AHEAD < NC)
        def _():
            start1(t + AHEAD)

        def stage(lag, fn, last=NC):
            j = t - lag

            @pl.when((j >= 0) & (j < last) & (lax.rem(j + 2 * NC, 2) == c))
            def _():
                fn(j)

        stage(2, reduce_one)
        stage(3, finish)
        j = t - 1

        @pl.when((j >= 0) & (j < NC))
        def _():
            multiply(j)

            @pl.when(lax.rem(j, 2) != c)
            def _():
                to_sibling(j).start()

        stage(2, reduce_two)
        stage(5, lambda j: forward_two(j // 2), 2 * QF)
        stage(4, lambda j: forward_one(j // 2), 2 * QF)
        return carry

    lax.fori_loop(1, NC + 3, step, 0)

    tile = top[:, pl.ds(0, 128)]
    for i in range(1, FFN // 128):
        tile = jnp.maximum(tile, top[:, pl.ds(128 * i, 128)])
    PK[k] = tile
    pcopies = []
    for i in range(1, 8):
        p = lax.rem(k + i, 8)
        pcopies.append(rc(PK.at[k], PK.at[k], ps.at[i - 1], pr.at[i - 1], (e, p)))
        pcopies[-1].start()
    for cp in gcopies(QF, 0):
        cp.start()
    for cp in pcopies:
        cp.wait_recv()
    peak = jnp.max(PK[...])
    pk_ref[...] = jnp.full((8, 128), peak, jnp.float32)
    shrink, factor = scale_factors(peak, 8)

    def put(start, first, n):
        rows = nm[pl.ds(first, n)].reshape(n // 8, 8, FFN)
        sl[pl.ds(start, n)] = ((rows * shrink) * factor).reshape(n, FFN).astype(jnp.bfloat16)

    for q in range(QF):
        put(LATE * q, 128 * q + EARLY, LATE)
    for q in range(QF, QN - 1):
        put(LATE * QF + 128 * (q - QF), 128 * q, 128)
    for cp in gcopies(QF + 1, 1):
        cp.start()
    put(LA, 128 * (QN - 1) + EARLY_LAST, LB)
    for cp in gcopies(QF + 2, 2):
        cp.start()
    for last in range(3):
        forward_one(QF + last, last)
    for last in range(3):
        forward_two(QF + last, last)

    def drain(g, last):
        blocks = (z, zm, zp, zo)
        for i in range(4):
            b = block(2 * blocks[i] + 1 - c, g, last)
            rc(b, b, gs.at[g, 4 + i], gr.at[g, 4 + i], sib).wait_recv()
        w = gcopies(g, last)
        for cp in w[:3] + fcopies(g, last):
            cp.wait_send()
        w[3].wait()

    for cp in pcopies:
        cp.wait_send()
    for g in range(QF):
        drain(g, None)
    for last in range(3):
        drain(QF + last, last)
    for q in range(QN):
        for cp in lcopies(q):
            cp.wait()
        for cp in zcopies(2 * q + c):
            cp.wait_send()
        to_sibling(2 * q + 1 - c).wait_send()

    def drain_sends(j, carry):
        for h in (0, 1):
            for i in range(3):
                a = R[h].at[j, :, 0]
                rc(a, a, s1.at[h, j, i], r1.at[h, j, i], sib).wait_send()
                a = R[h].at[j, 0]
                rc(a, a, s2.at[h, j, i], r2.at[h, j, i], sib).wait_send()
        return carry

    lax.fori_loop(0, NC, drain_sends, 0)


def exchange(out_grad, hidden, counts, master, m1, m2):
    V, DMA = pltpu.VMEM, pltpu.SemaphoreType.DMA
    f32, bf16 = jnp.float32, jnp.bfloat16
    any_spec = pl.BlockSpec(memory_space=pl.ANY)
    rows = master.shape[0]
    return pl.pallas_call(
        exchange_kernel,
        name="exchange",
        out_shape=(
            jax.ShapeDtypeStruct((8, EN, FFN), f32),
            jax.ShapeDtypeStruct((8, LN, FFN), bf16),
            jax.ShapeDtypeStruct((rows, FFN), f32),
            jax.ShapeDtypeStruct((rows, FFN), bf16),
            jax.ShapeDtypeStruct((rows, FFN), bf16),
            jax.ShapeDtypeStruct((8, 128), f32),
        ),
        in_specs=[any_spec, any_spec, pl.BlockSpec(memory_space=pltpu.SMEM), any_spec, any_spec, any_spec],
        out_specs=(any_spec,) * 5 + (pl.BlockSpec(memory_space=pltpu.VMEM),),
        scratch_shapes=[
            V((NC, 4, 4, 64, 512), bf16),
            V((NC, 4, 4, 32, 512), bf16),
            V((NC, 4, 4, 32, 512), bf16),
            V((1024, FFN), bf16),
            V((FFN, 1024), bf16),
            V((NC, 4, FFN, 128), f32),
            V((NC // 2, 4, FFN, 128), f32),
            V((NC // 2, 2, HALF, 128), f32),
            V((NC // 2, 2, FFN, 128), f32),
            V((rows, FFN), f32),
            V((rows, FFN), bf16),
            V((rows, FFN), bf16),
            V((rows, FFN), f32),
            V((rows, FFN), bf16),
            V((rows, FFN), bf16),
            V((LN, FFN), bf16),
            V((8, 8, 128), f32),
            V((8, FFN), f32),
            DMA((2, NC)),
            DMA((2, NC, 3)),
            DMA((2, NC, 3)),
            DMA((2, NC, 3)),
            DMA((2, NC, 3)),
            DMA((2, NC)),
            DMA((NC // 2,)),
            DMA((NC // 2,)),
            DMA((NC // 2, 6)),
            DMA((NC // 2, 6)),
            DMA((QN + 2, 8)),
            DMA((QN + 2, 8)),
            DMA((QN + 2,)),
            DMA((QN, 3)),
            DMA((4,)),
            DMA((7,)),
            DMA((7,)),
        ],
        compiler_params=pltpu.CompilerParams(
            collective_id=0, has_side_effects=True, vmem_limit_bytes=62 << 20
        ),
    )(out_grad.reshape(4, 4, 64, D), hidden, counts, master, m1, m2)


BLOCKS = 8
ROWS = D // BLOCKS


def scale_kernel(
    w_ref, sl_ref, nmi_ref, m1_ref, m2_ref, pk_ref,
    nm_ref, m1o_ref, m2o_ref, s_ref, peak_ref,
    wv, sv, v0, v1, v2, isem, lsem, osem, ssem,
):
    lc = pltpu.make_async_copy
    early = [(128 * q, EARLY * q, EARLY) for q in range(QF)] + [(128 * (QN - 1), EARLY * QF, EARLY_LAST)]
    late = [(128 * q + EARLY, LATE * q, LATE) for q in range(QF)] + [
        (128 * q, LATE * QF + 128 * (q - QF), 128) for q in range(QF, QN - 1)
    ] + [(128 * (QN - 1) + EARLY_LAST, LA, LB)]

    def load(b):
        return [lc(w_ref.at[b], wv.at[b], isem.at[b])] + [
            lc(sl_ref.at[b, pl.ds(o, n)], sv.at[b, pl.ds(r, n)], lsem.at[b, i]) for i, (r, o, n) in enumerate(late)
        ]

    small = (lc(nmi_ref, v0, ssem.at[0]), lc(m1_ref, v1, ssem.at[1]), lc(m2_ref, v2, ssem.at[2]))
    for cp in small:
        cp.start()
    for b in range(BLOCKS):
        for cp in load(b):
            cp.start()
    peak = jnp.max(pk_ref[...])
    peak_ref[0] = peak
    shrink, factor = scale_factors(peak, 8)
    outs = []
    for i, (v, o) in enumerate(((v0, nm_ref), (v1, m1o_ref), (v2, m2o_ref))):
        small[i].wait()
        outs.append(lc(v, o, osem.at[BLOCKS + i]))
        outs[-1].start()
    for b in range(BLOCKS):
        for cp in load(b):
            cp.wait()

        for r, o, n in early:
            v = wv[b, pl.ds(o, n)].reshape(n // 8, 8, FFN)
            sv[b, pl.ds(r, n)] = ((v * shrink) * factor).reshape(n, FFN).astype(jnp.bfloat16)
        outs.append(lc(sv.at[b], s_ref.at[pl.ds(b * ROWS, ROWS)], osem.at[b]))
        outs[-1].start()
    for cp in outs:
        cp.wait()


def scale(w, sl, nm, m1, m2, pk):
    V, DMA = pltpu.VMEM, pltpu.SemaphoreType.DMA
    f32, bf16 = jnp.float32, jnp.bfloat16
    any_spec = pl.BlockSpec(memory_space=pl.ANY)
    rows = m1.shape[0]
    return pl.pallas_call(
        scale_kernel,
        name="scale",
        out_shape=(
            jax.ShapeDtypeStruct((rows, FFN), f32),
            jax.ShapeDtypeStruct((rows, FFN), bf16),
            jax.ShapeDtypeStruct((rows, FFN), bf16),
            jax.ShapeDtypeStruct((D, FFN), bf16),
            jax.ShapeDtypeStruct((1,), f32),
        ),
        in_specs=[any_spec] * 5 + [pl.BlockSpec(memory_space=pltpu.VMEM)],
        out_specs=(any_spec,) * 4 + (pl.BlockSpec(memory_space=pltpu.SMEM),),
        scratch_shapes=[
            V((BLOCKS, EN, FFN), f32),
            V((BLOCKS, ROWS, FFN), bf16),
            V((rows, FFN), f32),
            V((rows, FFN), bf16),
            V((rows, FFN), bf16),
            DMA((BLOCKS,)),
            DMA((BLOCKS, QN)),
            DMA((BLOCKS + 3,)),
            DMA((3,)),
        ],
        compiler_params=pltpu.CompilerParams(vmem_limit_bytes=63 << 20),
    )(w, sl, nm, m1, m2, pk)


def local(out_grad, hidden_saved, recv_counts, master_weight, moment_one, moment_two):
    w, sl, nm, n1, n2, pk = exchange(
        out_grad, hidden_saved, recv_counts, master_weight, moment_one, moment_two
    )
    return scale(w, sl, nm, n1, n2, pk)


def solution(mesh):
    placed = (
        P(("expert", "edata"), None),
        P(("expert", "edata"), None),
        P(("expert", "edata")),
        P(("expert", "edata"), None),
        P(("expert", "edata"), None),
        P(("expert", "edata"), None),
    )
    return jax.shard_map(
        local,
        mesh=mesh,
        in_specs=placed,
        out_specs=(
            P(("expert", "edata"), None),
            P(("expert", "edata"), None),
            P(("expert", "edata"), None),
            P("expert", None),
            P("expert"),
        ),
        check_vma=False,
    )
```

```python
import functools

import jax
import jax.numpy as jnp
from jax import lax
from jax.experimental import pallas as pl
from jax.experimental.pallas import tpu as pltpu
from jax.sharding import PartitionSpec as P

MESH = pl.DeviceIdType.MESH

beta_one = 0.9
beta_two = 0.999
correct_one = 1.0 - 0.9**5
correct_two = 1.0 - 0.999**5
adam_eps = 1e-08
learn_rate = 0.05
weight_decay = 1.0
peak_eps = 1e-06

D = 4096
FFN = 768
HALF = FFN // 2
NC = 8
AHEAD = 2
QN = NC // 2
QF = 2
EARLY = 112
EARLY_LAST = 80
LATE = 128 - EARLY
EN = QF * EARLY + EARLY_LAST
LN = 128 * QN - EN
LA = QF * LATE + (QN - 1 - QF) * 128
LB = 128 - EARLY_LAST


def scale_factors(peak, rows):
    whole = jnp.full((rows, FFN), peak + peak_eps, jnp.float32)
    shrink = jnp.where(whole > 2.0**100, jnp.float32(2.0**-64), jnp.float32(1.0))
    return shrink, 1.0 / (whole * shrink)


def exchange_kernel(
    x_ref, h_ref, cnt_ref, mw_ref, m1_ref, m2_ref,
    w_ref, sl_ref, nmo_ref, m1o_ref, m2o_ref, pk_ref,
    F, RA, RB, H, HT, PB, DB, ZR, ZF, mw, m1, m2, nm, n1, n2, sl, PK, top,
    l1, s1, r1, s2, r2, l2, ds, dr, zs, zr, gs, gr, gl, ls, isem, ps, pr,
):
    e = lax.axis_index("expert")
    k = lax.axis_index("edata")
    y, x = e // 4, lax.rem(e, 4)
    z, c = k // 2, lax.rem(k, 2)
    zp, zm, zo = lax.rem(z + 1, 4), lax.rem(z + 3, 4), lax.rem(z + 2, 4)
    sib = (e, 2 * z + 1 - c)
    up = (e, 2 * zp + c)
    down = (e, 2 * zm + c)
    hops = (1, 3, 2)

    def xdev(p):
        return (y * 4 + p, k)

    def ydev(p):
        return (p * 4 + x, k)

    def rc(src, dst, ssem, rsem, dev):
        return pltpu.make_async_remote_copy(
            src_ref=src, dst_ref=dst, send_sem=ssem, recv_sem=rsem,
            device_id=dev, device_id_type=MESH,
        )

    lc = pltpu.make_async_copy

    barrier = pltpu.get_barrier_semaphore()
    for d in hops:
        pl.semaphore_signal(barrier, inc=1, device_id=xdev(lax.rem(x + d, 4)), device_id_type=MESH)
        pl.semaphore_signal(barrier, inc=1, device_id=ydev(lax.rem(y + d, 4)), device_id_type=MESH)
    for i in range(1, 8):
        dev = (e, lax.rem(k + i, 8))
        pl.semaphore_signal(barrier, inc=1, device_id=dev, device_id_type=MESH)

    ins = (
        lc(h_ref, H, isem.at[0]),
        lc(mw_ref, mw, isem.at[1]),
        lc(m1_ref, m1, isem.at[2]),
        lc(m2_ref, m2, isem.at[3]),
    )
    for cp in ins:
        cp.start()
    pl.semaphore_wait(barrier, 13)

    R = (RA, RB)
    own1 = (x, y)
    own2 = (y, x)

    def start1(j):
        base = 512 * lax.rem(j, 2) + 128 * (j // 2)

        def src(h, p, s):
            cols = pl.ds(pl.multiple_of(1024 * s + base, 128), 128)
            if h == 0:
                return x_ref.at[:, p, pl.ds(0, 32), cols]
            return x_ref.at[p, :, pl.ds(32, 32), cols]

        for i, d in enumerate(hops):
            for h in (0, 1):
                p = lax.rem(own1[h] + d, 4)
                for s in range(4):
                    rc(
                        src(h, p, s), R[h].at[j, :, own1[h], :, pl.ds(128 * s, 128)],
                        s1.at[h, j, i], r1.at[h, j, i], (xdev, ydev)[h](p),
                    ).start()
        for h in (0, 1):
            for s in range(4):
                lc(src(h, own1[h], s), R[h].at[j, :, own1[h], :, pl.ds(128 * s, 128)], l1.at[h, j]).start()

    def dst2(h, j):
        if h == 0:
            return F.at[j, y, :, pl.ds(0, 32)]
        return F.at[j, :, x, pl.ds(32, 32)]

    def start2(j):
        for h in (0, 1):
            mine = R[h].at[j, :, own1[h]]
            lc(mine, mine, l1.at[h, j]).wait()
            for i, d in enumerate(hops):
                got = R[h].at[j, :, lax.rem(own1[h] + 4 - d, 4)]
                rc(got, got, s1.at[h, j, i], r1.at[h, j, i], sib).wait_recv()
            for i, d in enumerate(hops):
                p = lax.rem(own2[h] + d, 4)
                rc(R[h].at[j, p], dst2(h, j), s2.at[h, j, i], r2.at[h, j, i], (ydev, xdev)[h](p)).start()
            lc(R[h].at[j, own2[h]], dst2(h, j), l2.at[h, j]).start()

    def got2(h, j, i):
        p = lax.rem(own2[h] + 4 - hops[i], 4)
        if h == 0:
            return F.at[j, p, :, pl.ds(0, 32)]
        return F.at[j, :, p, pl.ds(32, 32)]

    def multiply(j):
        for h in (0, 1):
            for i in range(3):
                g = got2(h, j, i)
                rc(g, g, s2.at[h, j, i], r2.at[h, j, i], sib).wait_recv()
            lc(R[h].at[j, own2[h]], dst2(h, j), l2.at[h, j]).wait()
        for n in range(2):
            a = F[j, :, :, :, pl.ds(256 * n, 256)].reshape(1024, 256)
            prod = jnp.dot(HT[...], a, preferred_element_type=jnp.float32)
            PB[j, 2 * n] = prod[:, :128]
            PB[j, 2 * n + 1] = prod[:, 128:]

    def to_sibling(j):
        return rc(PB.at[j], DB.at[j // 2], ds.at[j // 2], dr.at[j // 2], sib)

    def zcopies(j):
        q = j // 2
        lo, hi = pl.ds(0, HALF), pl.ds(HALF, HALF)
        return (
            rc(PB.at[j, zo, lo], ZR.at[q, 0], zs.at[q, 0], zr.at[q, 0], up),
            rc(PB.at[j, zo, hi], ZR.at[q, 1], zs.at[q, 1], zr.at[q, 1], down),
            rc(PB.at[j, zp, hi], ZF.at[q, 0, hi], zs.at[q, 2], zr.at[q, 2], up),
            rc(PB.at[j, zm, lo], ZF.at[q, 1, lo], zs.at[q, 3], zr.at[q, 3], down),
            rc(PB.at[j, zp, lo], ZF.at[q, 0, lo], zs.at[q, 4], zr.at[q, 4], up),
            rc(PB.at[j, zm, hi], ZF.at[q, 1, hi], zs.at[q, 5], zr.at[q, 5], down),
        )

    def reduce_one(j):
        q = j // 2
        to_sibling(j).wait_recv()
        cps = zcopies(j)
        PB[j, zo] = PB[j, zo] + DB[q, zo]
        cps[0].start()
        cps[1].start()
        PB[j, zp] = PB[j, zp] + DB[q, zp]
        cps[2].start()
        PB[j, zm] = PB[j, zm] + DB[q, zm]
        cps[3].start()
        PB[j, z] = PB[j, z] + DB[q, z]

    def reduce_two(j):
        q = j // 2
        cps = zcopies(j)
        cps[0].wait_recv()
        PB[j, zp, pl.ds(0, HALF)] = PB[j, zp, pl.ds(0, HALF)] + ZR[q, 0]
        cps[4].start()
        cps[1].wait_recv()
        PB[j, zm, pl.ds(HALF, HALF)] = PB[j, zm, pl.ds(HALF, HALF)] + ZR[q, 1]
        cps[5].start()

    def rows_of(q):
        return pl.ds(pl.multiple_of(128 * q, 128), 128)

    def part(g, last):
        if last is None:
            return w_ref, pl.multiple_of(EARLY * g, 8), EARLY, EARLY // 2
        return (
            (w_ref, QF * EARLY, EARLY_LAST, EARLY_LAST // 2),
            (sl_ref, 0, LA, LA // 32 * 16),
            (sl_ref, LA, LB, (LB + 31) // 32 * 16),
        )[last]

    def block(kk, g, last, piece=0):
        ref, off, n, cut = part(g, last)
        first, count = ((0, n), (0, cut), (cut, n - cut))[piece]
        return ref.at[kk, pl.ds(off + first, count)]

    def gcopies(g, last=None):
        if last is None:
            own = nm.at[pl.ds(pl.multiple_of(128 * g, 128), EARLY)]
        else:
            own = (nm.at[pl.ds(128 * (QN - 1), EARLY_LAST)], sl.at[pl.ds(0, LA)], sl.at[pl.ds(LA, LB)])[last]
        b = block(k, g, last)
        return (
            rc(own, b, gs.at[g, 0], gr.at[g, 0], up),
            rc(own, b, gs.at[g, 1], gr.at[g, 1], down),
            rc(own, b, gs.at[g, 4], gr.at[g, 4], sib),
            lc(own, b, gl.at[g]),
        )

    def lcopies(q):
        rows = rows_of(q)
        return (
            lc(nm.at[rows], nmo_ref.at[rows], ls.at[q, 0]),
            lc(n1.at[rows], m1o_ref.at[rows], ls.at[q, 1]),
            lc(n2.at[rows], m2o_ref.at[rows], ls.at[q, 2]),
        )

    def finish(j):
        q = j // 2
        cps = zcopies(j)
        cps[2].wait_recv()
        cps[3].wait_recv()
        cps[4].wait_recv()
        cps[5].wait_recv()
        grad = (PB[j, z] + ZF[q, 0] + ZF[q, 1]).T
        rows = pl.ds(pl.multiple_of(128 * q, 128), 128)
        first = beta_one * m1[rows].astype(jnp.float32) + (1.0 - beta_one) * grad
        second = beta_two * m2[rows].astype(jnp.float32) + (1.0 - beta_two) * grad * grad
        update = first / correct_one / (jnp.sqrt(second / correct_two) + adam_eps)
        weight = mw[rows]
        weight = weight - learn_rate * (update + weight_decay * weight)
        nm[rows] = weight

        @pl.when(q < QF)
        def _():
            for cp in gcopies(q):
                cp.start()

        size = jnp.abs(weight)
        most = size[:8]
        for i in range(1, 16):
            most = jnp.maximum(most, size[8 * i : 8 * i + 8])
        top[...] = jnp.maximum(top[...], most)
        n1[rows] = first.astype(jnp.bfloat16)
        n2[rows] = second.astype(jnp.bfloat16)
        for cp in lcopies(q):
            cp.start()

    def fcopies(g, last=None):
        km, kp, ko = 2 * zm + c, 2 * zp + c, 2 * zo + c
        lo, hi = block(km, g, last, 1), block(kp, g, last, 2)
        bm, bp, bo = block(km, g, last), block(kp, g, last), block(ko, g, last)
        return (
            rc(lo, lo, gs.at[g, 2], gr.at[g, 2], up),
            rc(hi, hi, gs.at[g, 3], gr.at[g, 3], down),
            rc(bm, bm, gs.at[g, 5], gr.at[g, 5], sib),
            rc(bp, bp, gs.at[g, 6], gr.at[g, 6], sib),
            rc(bo, bo, gs.at[g, 7], gr.at[g, 7], sib),
        )

    def forward_one(g, last=None):
        w, f = gcopies(g, last), fcopies(g, last)
        w[0].wait_recv()
        f[0].start()
        f[2].start()
        w[1].wait_recv()
        f[1].start()
        f[3].start()

    def forward_two(g, last=None):
        ko = 2 * zo + c
        f = fcopies(g, last)
        lo, hi = block(ko, g, last, 1), block(ko, g, last, 2)
        rc(lo, lo, gs.at[g, 2], gr.at[g, 2], up).wait_recv()
        rc(hi, hi, gs.at[g, 3], gr.at[g, 3], down).wait_recv()
        f[4].start()

    for j in range(AHEAD):
        start1(j)
    start2(0)
    start1(AHEAD)

    ins[0].wait()
    slot = lax.broadcasted_iota(jnp.int32, (64, FFN), 0)
    for s in range(8):
        parts = []
        for t in (2 * s, 2 * s + 1):
            rows = H[pl.ds(64 * t, 64)].astype(jnp.float32)
            parts.append(jnp.where(slot < cnt_ref[t], rows, 0.0))
        HT[:, pl.ds(128 * s, 128)] = jnp.concatenate(parts, axis=0).T.astype(jnp.bfloat16)
    for cp in ins[1:]:
        cp.wait()
    top[...] = jnp.zeros_like(top)

    def step(t, carry):
        @pl.when(t < NC)
        def _():
            start2(t)

        @pl.when(t + AHEAD < NC)
        def _():
            start1(t + AHEAD)

        def stage(lag, fn, last=NC):
            j = t - lag

            @pl.when((j >= 0) & (j < last) & (lax.rem(j + 2 * NC, 2) == c))
            def _():
                fn(j)

        stage(2, reduce_one)
        stage(3, finish)
        j = t - 1

        @pl.when((j >= 0) & (j < NC))
        def _():
            multiply(j)

            @pl.when(lax.rem(j, 2) != c)
            def _():
                to_sibling(j).start()

        stage(2, reduce_two)
        stage(5, lambda j: forward_two(j // 2), 2 * QF)
        stage(4, lambda j: forward_one(j // 2), 2 * QF)
        return carry

    lax.fori_loop(1, NC + 3, step, 0)

    tile = top[:, pl.ds(0, 128)]
    for i in range(1, FFN // 128):
        tile = jnp.maximum(tile, top[:, pl.ds(128 * i, 128)])
    PK[k] = tile
    pcopies = []
    for i in range(1, 8):
        p = lax.rem(k + i, 8)
        pcopies.append(rc(PK.at[k], PK.at[k], ps.at[i - 1], pr.at[i - 1], (e, p)))
        pcopies[-1].start()
    for cp in gcopies(QF, 0):
        cp.start()
    for cp in pcopies:
        cp.wait_recv()
    peak = jnp.max(PK[...])
    pk_ref[...] = jnp.full((8, 128), peak, jnp.float32)
    shrink, factor = scale_factors(peak, 8)

    def put(start, first, n):
        rows = nm[pl.ds(first, n)].reshape(n // 8, 8, FFN)
        sl[pl.ds(start, n)] = ((rows * shrink) * factor).reshape(n, FFN).astype(jnp.bfloat16)

    for q in range(QF):
        put(LATE * q, 128 * q + EARLY, LATE)
    for q in range(QF, QN - 1):
        put(LATE * QF + 128 * (q - QF), 128 * q, 128)
    for cp in gcopies(QF + 1, 1):
        cp.start()
    put(LA, 128 * (QN - 1) + EARLY_LAST, LB)
    for cp in gcopies(QF + 2, 2):
        cp.start()
    for last in range(3):
        forward_one(QF + last, last)
    for last in range(3):
        forward_two(QF + last, last)

    def drain(g, last):
        blocks = (z, zm, zp, zo)
        for i in range(4):
            b = block(2 * blocks[i] + 1 - c, g, last)
            rc(b, b, gs.at[g, 4 + i], gr.at[g, 4 + i], sib).wait_recv()
        w = gcopies(g, last)
        for cp in w[:3] + fcopies(g, last):
            cp.wait_send()
        w[3].wait()

    for cp in pcopies:
        cp.wait_send()
    for g in range(QF):
        drain(g, None)
    for last in range(3):
        drain(QF + last, last)
    for q in range(QN):
        for cp in lcopies(q):
            cp.wait()
        for cp in zcopies(2 * q + c):
            cp.wait_send()
        to_sibling(2 * q + 1 - c).wait_send()

    def drain_sends(j, carry):
        for h in (0, 1):
            for i in range(3):
                a = R[h].at[j, :, 0]
                rc(a, a, s1.at[h, j, i], r1.at[h, j, i], sib).wait_send()
                a = R[h].at[j, 0]
                rc(a, a, s2.at[h, j, i], r2.at[h, j, i], sib).wait_send()
        return carry

    lax.fori_loop(0, NC, drain_sends, 0)


def exchange(out_grad, hidden, counts, master, m1, m2):
    V, DMA = pltpu.VMEM, pltpu.SemaphoreType.DMA
    f32, bf16 = jnp.float32, jnp.bfloat16
    any_spec = pl.BlockSpec(memory_space=pl.ANY)
    rows = master.shape[0]
    return pl.pallas_call(
        exchange_kernel,
        name="exchange",
        out_shape=(
            jax.ShapeDtypeStruct((8, EN, FFN), f32),
            jax.ShapeDtypeStruct((8, LN, FFN), bf16),
            jax.ShapeDtypeStruct((rows, FFN), f32),
            jax.ShapeDtypeStruct((rows, FFN), bf16),
            jax.ShapeDtypeStruct((rows, FFN), bf16),
            jax.ShapeDtypeStruct((8, 128), f32),
        ),
        in_specs=[any_spec, any_spec, pl.BlockSpec(memory_space=pltpu.SMEM), any_spec, any_spec, any_spec],
        out_specs=(any_spec,) * 5 + (pl.BlockSpec(memory_space=pltpu.VMEM),),
        scratch_shapes=[
            V((NC, 4, 4, 64, 512), bf16),
            V((NC, 4, 4, 32, 512), bf16),
            V((NC, 4, 4, 32, 512), bf16),
            V((1024, FFN), bf16),
            V((FFN, 1024), bf16),
            V((NC, 4, FFN, 128), f32),
            V((NC // 2, 4, FFN, 128), f32),
            V((NC // 2, 2, HALF, 128), f32),
            V((NC // 2, 2, FFN, 128), f32),
            V((rows, FFN), f32),
            V((rows, FFN), bf16),
            V((rows, FFN), bf16),
            V((rows, FFN), f32),
            V((rows, FFN), bf16),
            V((rows, FFN), bf16),
            V((LN, FFN), bf16),
            V((8, 8, 128), f32),
            V((8, FFN), f32),
            DMA((2, NC)),
            DMA((2, NC, 3)),
            DMA((2, NC, 3)),
            DMA((2, NC, 3)),
            DMA((2, NC, 3)),
            DMA((2, NC)),
            DMA((NC // 2,)),
            DMA((NC // 2,)),
            DMA((NC // 2, 6)),
            DMA((NC // 2, 6)),
            DMA((QN + 2, 8)),
            DMA((QN + 2, 8)),
            DMA((QN + 2,)),
            DMA((QN, 3)),
            DMA((4,)),
            DMA((7,)),
            DMA((7,)),
        ],
        compiler_params=pltpu.CompilerParams(
            collective_id=0, has_side_effects=True, vmem_limit_bytes=62 << 20
        ),
    )(out_grad.reshape(4, 4, 64, D), hidden, counts, master, m1, m2)


BLOCKS = 8
ROWS = D // BLOCKS


def scale_kernel(
    w_ref, sl_ref, nmi_ref, m1_ref, m2_ref, pk_ref,
    nm_ref, m1o_ref, m2o_ref, s_ref, peak_ref,
    wv, sv, v0, v1, v2, isem, lsem, osem, ssem,
):
    lc = pltpu.make_async_copy
    early = [(128 * q, EARLY * q, EARLY) for q in range(QF)] + [(128 * (QN - 1), EARLY * QF, EARLY_LAST)]
    late = [(128 * q + EARLY, LATE * q, LATE) for q in range(QF)] + [
        (128 * q, LATE * QF + 128 * (q - QF), 128) for q in range(QF, QN - 1)
    ] + [(128 * (QN - 1) + EARLY_LAST, LA, LB)]

    def load(b):
        return [lc(w_ref.at[b], wv.at[b], isem.at[b])] + [
            lc(sl_ref.at[b, pl.ds(o, n)], sv.at[b, pl.ds(r, n)], lsem.at[b, i]) for i, (r, o, n) in enumerate(late)
        ]

    small = (lc(nmi_ref, v0, ssem.at[0]), lc(m1_ref, v1, ssem.at[1]), lc(m2_ref, v2, ssem.at[2]))
    for cp in small:
        cp.start()
    for b in range(BLOCKS):
        for cp in load(b):
            cp.start()
    peak = jnp.max(pk_ref[...])
    peak_ref[0] = peak
    shrink, factor = scale_factors(peak, 8)
    outs = []
    for i, (v, o) in enumerate(((v0, nm_ref), (v1, m1o_ref), (v2, m2o_ref))):
        small[i].wait()
        outs.append(lc(v, o, osem.at[BLOCKS + i]))
        outs[-1].start()
    for b in range(BLOCKS):
        for cp in load(b):
            cp.wait()

        for r, o, n in early:
            v = wv[b, pl.ds(o, n)].reshape(n // 8, 8, FFN)
            sv[b, pl.ds(r, n)] = ((v * shrink) * factor).reshape(n, FFN).astype(jnp.bfloat16)
        outs.append(lc(sv.at[b], s_ref.at[pl.ds(b * ROWS, ROWS)], osem.at[b]))
        outs[-1].start()
    for cp in outs:
        cp.wait()


def scale(w, sl, nm, m1, m2, pk):
    V, DMA = pltpu.VMEM, pltpu.SemaphoreType.DMA
    f32, bf16 = jnp.float32, jnp.bfloat16
    any_spec = pl.BlockSpec(memory_space=pl.ANY)
    rows = m1.shape[0]
    return pl.pallas_call(
        scale_kernel,
        name="scale",
        out_shape=(
            jax.ShapeDtypeStruct((rows, FFN), f32),
            jax.ShapeDtypeStruct((rows, FFN), bf16),
            jax.ShapeDtypeStruct((rows, FFN), bf16),
            jax.ShapeDtypeStruct((D, FFN), bf16),
            jax.ShapeDtypeStruct((1,), f32),
        ),
        in_specs=[any_spec] * 5 + [pl.BlockSpec(memory_space=pltpu.VMEM)],
        out_specs=(any_spec,) * 4 + (pl.BlockSpec(memory_space=pltpu.SMEM),),
        scratch_shapes=[
            V((BLOCKS, EN, FFN), f32),
            V((BLOCKS, ROWS, FFN), bf16),
            V((rows, FFN), f32),
            V((rows, FFN), bf16),
            V((rows, FFN), bf16),
            DMA((BLOCKS,)),
            DMA((BLOCKS, QN)),
            DMA((BLOCKS + 3,)),
            DMA((3,)),
        ],
        compiler_params=pltpu.CompilerParams(vmem_limit_bytes=63 << 20),
    )(w, sl, nm, m1, m2, pk)


def local(out_grad, hidden_saved, recv_counts, master_weight, moment_one, moment_two):
    w, sl, nm, n1, n2, pk = exchange(
        out_grad, hidden_saved, recv_counts, master_weight, moment_one, moment_two
    )
    return scale(w, sl, nm, n1, n2, pk)


def solution(mesh):
    placed = (
        P(("expert", "edata"), None),
        P(("expert", "edata"), None),
        P(("expert", "edata")),
        P(("expert", "edata"), None),
        P(("expert", "edata"), None),
        P(("expert", "edata"), None),
    )
    return jax.shard_map(
        local,
        mesh=mesh,
        in_specs=placed,
        out_specs=(
            P(("expert", "edata"), None),
            P(("expert", "edata"), None),
            P(("expert", "edata"), None),
            P("expert", None),
            P("expert"),
        ),
        check_vma=False,
    )
```
